768 devices in a mesh: sec: 12 (over x, z_hi), lat: 64 (over z_lo, y, core).
Axes of the slice: x: 4, y: 8, z: 12 (z_hi: 3, z_lo: 4; z = z_hi * 4 + z_lo), core: 2. Of those that a mesh axis runs over, the one named last changes fastest.
Arguments:
- spectra: float32 [256, 288, 768], P('lat', 'sec'), may hold values from 0.2 to 2
- turning: float32 [256, 288], P('lat', 'sec'), may hold values from -0.45 to 0.45
- currents: float32 [256, 288, 64], P('lat', 'sec'), may hold values from -3 to 3
- drag_rates: float32 [32], replicated, may hold values from 0.02 to 0.3
- land_mask: int32 [256, 288], P('lat', 'sec'), may hold values 0 or 1
- ocean_target: int32 [256, 288], P('lat', 'sec'), may hold values from 0 to 11, as said below
Outputs:
- spectra_out: float32 [256, 288, 768], P('lat', 'sec')
- currents_out: float32 [256, 288, 64], P('lat', 'sec')
The draws below stay inside these ranges and needn't reach their ends.
Inputs may be any that keep to these rules, and one draw needn't show every extreme that they name: `ocean_target`: in each device's block of 4 x 24 columns every target value appears on exactly 8 columns.
All inputs are finite; a program needn't handle non-finite values. No bound on the sum of `land_mask` on one device may be relied on, other than what follows from the above.
Results may differ from the reference program's by a relative error of at most 0.0003.
Values sent between devices are 32-bit elements; how exact they have to be, the bound alone decides.
A program may use at most 32 MiB of HBM per device.

```python
import math
import jax
import jax.numpy as jnp
from jax import lax

NFREQ = 24
NDIR = 32
NDEPTH = 32
LAT_DEV = 4
LON_DEV = 24
STEPS = 3
NLAT = 256
NLON = 288
N_SEC = 12
N_LAT = 64


def draw_ocean_target(key, part):
    column_count = LAT_DEV * LON_DEV
    band_count = NLAT // LAT_DEV
    sections = NLON // LON_DEV
    labels = jnp.arange(column_count, dtype=jnp.int32) % sections
    scores = jax.random.randint(key, (band_count * sections, column_count), 0, 32768, dtype=jnp.int32) * column_count + jnp.arange(column_count, dtype=jnp.int32)[None, :]
    shuffle = jnp.argsort(scores, axis=1, stable=True)
    values = labels[shuffle]
    return values.reshape(band_count, sections, LAT_DEV, LON_DEV).transpose(0, 2, 1, 3).reshape(NLAT, NLON)


def plant(result, key, least, top_value):
    place = [jax.random.randint(jax.random.fold_in(key, axis), (), 0, length) for axis, length in enumerate(result.shape)]
    main_axis = result.shape.index(max(result.shape))
    beside = place[:main_axis] + [(place[main_axis] + 1) % result.shape[main_axis]] + place[main_axis + 1:]
    return result.at[tuple(place)].set(least).at[tuple(beside)].set(top_value)


def block_levels(rng, dims, cuts, least, high):
    def one(dim, shards_of):
        draws = jax.random.uniform(jax.random.fold_in(jax.random.fold_in(rng, 6), dim), (shards_of,), jnp.float32, least / len(cuts), high / len(cuts))
        return jnp.repeat(jnp.exp(draws), dims[dim] // shards_of).reshape((-1,) + (1,) * (len(dims) - dim - 1))

    factor_of = one(*cuts[0])
    for cut in cuts[1:]:
        factor_of = factor_of * one(*cut)
    return factor_of


def gaussian(own_key, shape, width, bound, cuts=(), held_as=jnp.bfloat16):
    entries = width * jax.random.normal(own_key, shape, jnp.float32)
    if cuts:
        entries = entries * block_levels(own_key, shape, cuts, -0.22, 0.18)
    return jnp.clip(entries, -bound, bound).astype(held_as)


def setup_inputs(seed: int = 0) -> dict:
    seeds = jax.random.split(jax.random.key(seed), 7)
    return {
        "spectra": jnp.clip(jnp.exp(math.log(2.0) - 2.3025851 * jax.random.uniform(seeds[0], (NLAT, NLON, NFREQ * NDIR), jnp.float32) ** block_levels(seeds[0], (NLAT, NLON, NFREQ * NDIR), ((0, 64), (1, 12)), -0.2, 0.2)), 0.2, 2.0),
        "turning": jnp.clip(jax.random.uniform(seeds[1], (NLAT, NLON), jnp.float32, -0.45, 0.45) * block_levels(seeds[1], (NLAT, NLON), ((0, 64), (1, 12)), -0.4, 0.0), -0.45, 0.45),
        "currents": gaussian(seeds[2], (NLAT, NLON, 2 * NDEPTH), 0.5, 3.0, ((0, 64), (1, 12)), jnp.float32),
        "drag_rates": jnp.clip(jnp.exp(jax.random.uniform(seeds[3], (NDEPTH,), jnp.float32, math.log(0.02), math.log(0.3))), 0.02, 0.3),
        "land_mask": plant((jax.random.randint(seeds[4], (NLAT, NLON), 0, 8) < 7).astype(jnp.int32), jax.random.fold_in(seeds[4], 1), 0, 1),
        "ocean_target": draw_ocean_target(jax.random.fold_in(seeds[6], 71), 0),
    }


stokes_scale = 0.1
ocean_dt = 0.3
current_gain = 0.2


def build_tables(nfreq, ndir, ndepth):
    fraction = jnp.arange(nfreq, dtype=jnp.float32) / (nfreq - 1)
    angles = (jnp.arange(ndir, dtype=jnp.float32) + 0.5) * (2.0 * math.pi / ndir)
    east_part = jnp.cos(angles)
    north_part = jnp.sin(angles)
    courant = 0.1 + 0.3 * fraction
    levels = jnp.arange(ndepth, dtype=jnp.float32)
    depth_level = 0.5 + (ndepth - 2) * (1.0 - fraction)
    weights = jnp.maximum(1.0 - jnp.abs(levels[None, :] - depth_level[:, None]), 0.0)
    mean_weights = weights / jnp.sum(weights, axis=1, keepdims=True)
    x_rate = (courant[:, None] * east_part[None, :]).reshape(-1)
    y_rate = (courant[:, None] * north_part[None, :]).reshape(-1)
    compass = jnp.stack([east_part, north_part])
    eye_freq = jnp.eye(nfreq, dtype=jnp.float32)
    eye_two = jnp.eye(2, dtype=jnp.float32)
    stokes_matrix = (stokes_scale * weights[:, None, None, :] * compass.T[None, :, :, None]).reshape(nfreq * ndir, 2 * ndepth)
    moment_matrix = (eye_freq[:, None, None, :] * compass.T[None, :, :, None]).reshape(nfreq * ndir, 2 * nfreq)
    profile_matrix = (stokes_scale * eye_two[:, None, :, None] * weights[None, :, None, :]).reshape(2 * nfreq, 2 * ndepth)
    average_matrix = (eye_two[:, None, :, None] * mean_weights.T[None, :, None, :]).reshape(2 * ndepth, 2 * nfreq)
    turn_gain = 1.0 - 0.5 * fraction
    growth = current_gain * (1.0 + fraction)
    return (east_part, north_part, x_rate, y_rate, stokes_matrix, moment_matrix, profile_matrix,
            average_matrix, turn_gain, growth)


def upwind(center, west, east, south, north, x_rate, y_rate):
    along_x = jnp.maximum(x_rate, 0.0) * (center - west) + jnp.minimum(x_rate, 0.0) * (east - center)
    along_y = jnp.maximum(y_rate, 0.0) * (center - south) + jnp.minimum(y_rate, 0.0) * (north - center)
    return center - along_x - along_y


def turn_grow(advected, turning, current_eff, east_part, north_part, turn_gain, growth, nfreq, ndir):
    layout = advected.shape
    spread = advected.reshape(layout[:-1] + (nfreq, ndir))
    turn_rate = turning[..., None, None] * turn_gain[:, None]
    behind = jnp.roll(spread, 1, axis=-1)
    forward = jnp.roll(spread, -1, axis=-1)
    turned = spread - jnp.maximum(turn_rate, 0.0) * (spread - behind) - jnp.minimum(turn_rate, 0.0) * (forward - spread)
    zonal = current_eff[..., :nfreq]
    meridional = current_eff[..., nfreq:]
    aligned = zonal[..., None] * east_part + meridional[..., None] * north_part
    grown = turned * (1.0 + growth[:, None] * aligned)
    return grown.reshape(layout)


def ocean_step(currents, padded, stokes, coriolis, keep, ndepth):
    zonal = currents[..., :ndepth]
    meridional = currents[..., ndepth:]
    shear = 0.5 * (padded[1:-1, 2:, ndepth:] - padded[1:-1, :-2, ndepth:]) - 0.5 * (padded[2:, 1:-1, :ndepth] - padded[:-2, 1:-1, :ndepth])
    spin = coriolis[:, None, None] + shear
    new_zonal = keep * (zonal + ocean_dt * spin * (meridional + stokes[..., ndepth:]))
    new_merid = keep * (meridional - ocean_dt * spin * (zonal + stokes[..., :ndepth]))
    return jnp.concatenate([new_zonal, new_merid], axis=-1)


def to_blocks(field):
    trailing = field.shape[-1]
    split = field.reshape(N_LAT, LAT_DEV, N_SEC, LON_DEV, trailing)
    return split.transpose(0, 2, 1, 3, 4).reshape(N_LAT, N_SEC, LAT_DEV * LON_DEV, trailing)


def from_blocks(blocks):
    trailing = blocks.shape[-1]
    split = blocks.reshape(N_LAT, N_SEC, LAT_DEV, LON_DEV, trailing)
    return split.transpose(0, 2, 1, 3, 4).reshape(NLAT, NLON, trailing)


def swap_sections(blocks):
    trailing = blocks.shape[-1]
    per_target = LAT_DEV * LON_DEV // N_SEC
    grouped = blocks.reshape(N_LAT, N_SEC, N_SEC, per_target, trailing)
    return jnp.swapaxes(grouped, 1, 2).reshape(N_LAT, N_SEC, LAT_DEV * LON_DEV, trailing)


def reference(spectra, turning, currents, drag_rates, land_mask, ocean_target):
    (east_part, north_part, x_rate, y_rate, stokes_matrix, moment_matrix, profile_matrix,
     average_matrix, turn_gain, growth) = build_tables(NFREQ, NDIR, NDEPTH)
    order = jnp.argsort(to_blocks(ocean_target[..., None])[..., 0], axis=-1, stable=True)
    inverse = jnp.argsort(order, axis=-1, stable=True)
    sea = land_mask.astype(jnp.float32)[..., None]
    keep = 1.0 - drag_rates
    coriolis = 0.2 + 0.6 * jnp.arange(NLAT, dtype=jnp.float32) / NLAT
    for iteration in range(STEPS):
        stokes_wave = jnp.dot(spectra.reshape(-1, NFREQ * NDIR), stokes_matrix,
                              precision=lax.Precision.HIGHEST).reshape(NLAT, NLON, 2 * NDEPTH)
        sorted_stokes = jnp.take_along_axis(to_blocks(stokes_wave), order[..., None], axis=2)
        stokes = from_blocks(swap_sections(sorted_stokes))
        at_waves = jnp.take_along_axis(swap_sections(to_blocks(currents)), inverse[..., None], axis=2)
        current_eff = jnp.dot(from_blocks(at_waves).reshape(-1, 2 * NDEPTH), average_matrix,
                              precision=lax.Precision.HIGHEST).reshape(NLAT, NLON, 2 * NFREQ)
        padded = jnp.pad(spectra, ((1, 1), (1, 1), (0, 0)))
        advected = upwind(spectra, padded[1:-1, :-2], padded[1:-1, 2:], padded[:-2, 1:-1], padded[2:, 1:-1], x_rate, y_rate)
        new_spectra = turn_grow(advected, turning, current_eff, east_part, north_part, turn_gain, growth, NFREQ, NDIR) * sea
        ocean_padded = jnp.pad(currents, ((1, 1), (1, 1), (0, 0)))
        currents = ocean_step(currents, ocean_padded, stokes, coriolis, keep, NDEPTH) * sea
        spectra = new_spectra
    return (spectra, currents)
```

```python
import math

import jax
import jax.numpy as jnp
import ml_dtypes
import numpy as np
from jax import lax
from jax.experimental import pallas as pl
from jax.experimental.pallas import tpu as pltpu
from jax.sharding import PartitionSpec as P

NFREQ = 24
NDIR = 32
NDEPTH = 32
STEPS = 3
ROWS = 4
COLS = 24
CELLS = ROWS * COLS
SPEC = NFREQ * NDIR
WIDE = SPEC + 128

STOKES_SCALE = 0.1
OCEAN_DT = 0.3
CURRENT_GAIN = 0.2

MESH = pl.DeviceIdType.MESH


def halves(table):
    high = table.astype(ml_dtypes.bfloat16)
    low = (table - high.astype(np.float32)).astype(ml_dtypes.bfloat16)
    return high, low


def build_tables():
    f32 = np.float32
    fraction = np.arange(NFREQ, dtype=f32) / f32(NFREQ - 1)
    angles = (np.arange(NDIR, dtype=f32) + f32(0.5)) * f32(2.0 * math.pi / NDIR)
    east = np.cos(angles).astype(f32)
    north = np.sin(angles).astype(f32)
    compass = np.stack([east, north])
    courant = f32(0.1) + f32(0.3) * fraction
    depth_level = f32(0.5) + f32(NDEPTH - 2) * (f32(1.0) - fraction)
    levels = np.arange(NDEPTH, dtype=f32)
    weights = np.maximum(f32(1.0) - np.abs(levels[None, :] - depth_level[:, None]), f32(0.0))
    mean_weights = weights / np.sum(weights, axis=1, keepdims=True)
    x_rate = (courant[:, None] * east[None, :]).reshape(-1)
    y_rate = (courant[:, None] * north[None, :]).reshape(-1)
    turn_gain = f32(1.0) - f32(0.5) * fraction
    growth = f32(CURRENT_GAIN) * (f32(1.0) + fraction)
    stokes = (
        f32(STOKES_SCALE) * weights[:, None, None, :] * compass.T[None, :, :, None]
    ).reshape(SPEC, 2 * NDEPTH)
    swell = (
        growth[None, None, :, None] * mean_weights.T[None, :, :, None] * compass[:, None, None, :]
    ).reshape(2 * NDEPTH, SPEC)
    rates = np.zeros((8, SPEC), f32)
    rates[0] = f32(1.0) - np.abs(x_rate) - np.abs(y_rate)
    rates[1] = np.abs(x_rate)
    rates[2] = np.abs(y_rate)
    rates[3] = np.repeat(turn_gain, NDIR)
    stokes_table = np.concatenate(halves(stokes), axis=1)
    swell_high, swell_low = halves(swell)
    swell_table = np.concatenate([swell_high, swell_high, swell_low], axis=0)
    return rates, stokes_table, swell_table


def iota(shape, dim):
    return lax.broadcasted_iota(jnp.int32, shape, dim)


def round_half(x):
    return x.astype(jnp.bfloat16).astype(jnp.float32)


def kernel(
    sections,
    bands,
    spectra_hbm,
    turning_ref,
    currents_ref,
    drag_ref,
    land_ref,
    target_ref,
    rates_ref,
    stokes_hbm,
    swell_hbm,
    spectra_out,
    currents_out,
    state,
    south_halo,
    north_halo,
    west_halo,
    east_halo,
    west_edge,
    east_edge,
    outgoing,
    arrived,
    turned,
    stokes_table,
    swell_table,
    tiny,
    turn_size,
    turn_sign,
    sea,
    load_sem,
    lat_send,
    lat_recv,
    sec_send,
    sec_recv,
    pair_send,
    pair_recv,
):
    f32, bf16 = jnp.float32, jnp.bfloat16
    share = CELLS // sections
    sec = lax.axis_index("sec")
    lat = lax.axis_index("lat")
    has_west, has_east = sec > 0, sec < sections - 1
    has_south, has_north = lat > 0, lat < bands - 1

    loads = [
        pltpu.make_async_copy(spectra_hbm, state.at[0, :, pl.ds(0, SPEC)], load_sem.at[0]),
        pltpu.make_async_copy(stokes_hbm, stokes_table, load_sem.at[1]),
        pltpu.make_async_copy(swell_hbm, swell_table, load_sem.at[2]),
    ]
    for load in loads:
        load.start()

    barrier = pltpu.get_barrier_semaphore()
    for ahead in range(1, sections):
        peer = lax.rem(sec + ahead, sections)
        pl.semaphore_signal(barrier, inc=1, device_id={"sec": peer}, device_id_type=MESH)

    @pl.when(has_south)
    def _():
        pl.semaphore_signal(barrier, inc=1, device_id={"lat": lat - 1}, device_id_type=MESH)

    @pl.when(has_north)
    def _():
        pl.semaphore_signal(barrier, inc=1, device_id={"lat": lat + 1}, device_id_type=MESH)

    @pl.when(jnp.logical_not(has_south))
    def _():
        south_halo[...] = jnp.zeros_like(south_halo)

    @pl.when(jnp.logical_not(has_north))
    def _():
        north_halo[...] = jnp.zeros_like(north_halo)

    @pl.when(jnp.logical_not(has_west))
    def _():
        west_halo[...] = jnp.zeros_like(west_halo)

    @pl.when(jnp.logical_not(has_east))
    def _():
        east_halo[...] = jnp.zeros_like(east_halo)

    tiny[...] = jnp.zeros_like(tiny)
    tiny[0, 0:ROWS, 0:COLS] = turning_ref[...]
    tiny[1, 0:ROWS, 0:COLS] = land_ref[...].astype(f32)
    tiny[2, 0:ROWS, 0:COLS] = target_ref[...].astype(f32)
    tiny[3, 0:1, 0:NDEPTH] = 1.0 - drag_ref[...]
    lane_row = iota((1, 128), 1)
    target_rows = tiny[2]
    targets = jnp.full((1, 128), 99.0, f32)
    for y in range(ROWS):
        row = target_rows[y : y + 1, :]
        moved = pltpu.roll(row, COLS * y, 1) if y else row
        inside = jnp.logical_and(lane_row >= COLS * y, lane_row < COLS * (y + 1))
        targets = jnp.where(inside, moved, targets)
    matches = (iota((16, 128), 0).astype(f32) == targets).astype(f32)
    earlier = (iota((128, 128), 0) < iota((128, 128), 1)).astype(f32)
    before = jnp.dot(matches.astype(bf16), earlier.astype(bf16), preferred_element_type=f32)
    rank = jnp.sum(matches * before, axis=0, keepdims=True)
    place_of = targets * share + rank
    place = (iota((128, 128), 0).astype(f32) == place_of).astype(f32)
    place_back = jnp.transpose(place)[0:CELLS, 0:CELLS].astype(bf16)
    place = place[0:CELLS, 0:CELLS].astype(bf16)

    turn_columns = jnp.transpose(tiny[0])
    sea_columns = jnp.transpose(tiny[1])
    for y in range(ROWS):
        rows = slice(COLS * y, COLS * (y + 1))
        turn = jnp.broadcast_to(turn_columns[0:COLS, y : y + 1], (COLS, 128))
        turn_size[rows, :] = jnp.abs(turn)
        turn_sign[rows, :] = turn
        sea[rows, :] = jnp.broadcast_to(sea_columns[0:COLS, y : y + 1], (COLS, 128))

    keep = tiny[3, 0:1, :]
    keep = keep + pltpu.roll(keep, 32, 1)
    keep = keep + pltpu.roll(keep, 64, 1)

    lane = iota((COLS, 128), 1)
    line = iota((COLS, 128), 0)
    first_column = line == 0
    last_column = line == COLS - 1
    direction = lane & (NDIR - 1)
    goes_east = jnp.logical_or(direction < NDIR // 4, direction >= 3 * NDIR // 4)
    goes_north = direction < NDIR // 2
    first_direction = direction == 0
    last_direction = direction == NDIR - 1
    zonal = (lane & 63) < 32
    low_half = iota((CELLS, 128), 1) < 64
    twist = jnp.where(zonal, OCEAN_DT, -OCEAN_DT)

    def edge_rows(step):
        for y in range(ROWS):
            west_edge[step, y : y + 1, :] = state[step, COLS * y : COLS * y + 1, :]
            east_edge[step, y : y + 1, :] = state[step, COLS * (y + 1) - 1 : COLS * (y + 1), :]

    def to_south(step):
        return pltpu.make_async_remote_copy(
            src_ref=state.at[step, pl.ds(0, COLS)],
            dst_ref=north_halo.at[step],
            send_sem=lat_send.at[step, 0],
            recv_sem=lat_recv.at[step, 0],
            device_id={"lat": lat - 1},
            device_id_type=MESH,
        )

    def to_north(step):
        return pltpu.make_async_remote_copy(
            src_ref=state.at[step, pl.ds(CELLS - COLS, COLS)],
            dst_ref=south_halo.at[step],
            send_sem=lat_send.at[step, 1],
            recv_sem=lat_recv.at[step, 1],
            device_id={"lat": lat + 1},
            device_id_type=MESH,
        )

    def to_west(step):
        return pltpu.make_async_remote_copy(
            src_ref=west_edge.at[step],
            dst_ref=east_halo.at[step],
            send_sem=sec_send.at[step, 0],
            recv_sem=sec_recv.at[step, 0],
            device_id={"sec": sec - 1},
            device_id_type=MESH,
        )

    def to_east(step):
        return pltpu.make_async_remote_copy(
            src_ref=east_edge.at[step],
            dst_ref=west_halo.at[step],
            send_sem=sec_send.at[step, 1],
            recv_sem=sec_recv.at[step, 1],
            device_id={"sec": sec + 1},
            device_id_type=MESH,
        )

    def each_halo(step, act):
        for there, copy in ((has_west, to_west), (has_east, to_east), (has_south, to_south), (has_north, to_north)):

            @pl.when(there)
            def _():
                act(copy(step))

    def receive_halos(step):
        for there, copy in ((has_east, to_west), (has_west, to_east), (has_north, to_south), (has_south, to_north)):

            @pl.when(there)
            def _():
                copy(step).wait_recv()

    def pair_copy(step, ahead, source):
        peer = lax.rem(sec + ahead, sections)
        slot = lax.rem(sec + sections - ahead, sections) if source else sec
        return pltpu.make_async_remote_copy(
            src_ref=outgoing.at[step, peer],
            dst_ref=arrived.at[step, slot],
            send_sem=pair_send.at[step, ahead],
            recv_sem=pair_recv.at[step, slot],
            device_id={"sec": peer},
            device_id_type=MESH,
        )

    def stokes_part(values, chunk):
        high = values.astype(bf16)
        low = (values - high.astype(f32)).astype(bf16)
        both = jnp.concatenate([high, low], axis=0)
        return jnp.dot(both, stokes_table[256 * chunk : 256 * (chunk + 1), :], preferred_element_type=f32)

    def pack(step, drift):
        drift = drift[0:CELLS] + drift[CELLS:]
        drift = drift + pltpu.roll(drift, 64, 1)
        high = round_half(drift)
        pieces = jnp.where(low_half, high, drift - high).astype(bf16)
        drift = jnp.dot(place, pieces, preferred_element_type=f32)
        drift = drift + pltpu.roll(drift, 64, 1)
        message = jnp.where(low_half, drift, state[step, :, SPEC:WIDE])
        outgoing[step] = message.reshape(sections, share, 128)

    def send_pairs(step):
        for ahead in range(1, sections):
            pair_copy(step, ahead, False).start()
        arrived[step, sec] = outgoing[step, sec]

    flows = currents_ref[...].reshape(CELLS, 2 * NDEPTH)
    state[0, :, SPEC:WIDE] = jnp.concatenate([flows, flows], axis=1)
    loads[0].wait()
    edge_rows(0)
    loads[1].wait()
    drift = stokes_part(state[0, :, 0:256], 0)
    for chunk in (1, 2):
        drift = drift + stokes_part(state[0, :, 256 * chunk : 256 * (chunk + 1)], chunk)
    pack(0, drift)
    loads[2].wait()

    greeted = sections - 1 + has_south.astype(jnp.int32) + has_north.astype(jnp.int32)
    pl.semaphore_wait(barrier, greeted)
    send_pairs(0)
    each_halo(0, lambda copy: copy.start())

    global_row = (lat * ROWS).astype(f32)

    for step in range(STEPS):
        last = step == STEPS - 1
        receive_halos(step)

        for chunk in range(SPEC // 128):
            lanes = slice(128 * chunk, 128 * (chunk + 1))
            stay = rates_ref[0:1, lanes]
            rate_x = rates_ref[1:2, lanes]
            rate_y = rates_ref[2:3, lanes]
            gain = rates_ref[3:4, lanes]
            for y in range(ROWS):
                rows = slice(COLS * y, COLS * (y + 1))
                here = state[step, rows, lanes]
                west = jnp.where(first_column, west_halo[step, y : y + 1, lanes], pltpu.roll(here, 1, 0))
                east = jnp.where(last_column, east_halo[step, y : y + 1, lanes], pltpu.roll(here, COLS - 1, 0))
                south = state[step, COLS * (y - 1) : COLS * y, lanes] if y else south_halo[step, :, lanes]
                north = (
                    state[step, COLS * (y + 1) : COLS * (y + 2), lanes]
                    if y < ROWS - 1
                    else north_halo[step, :, lanes]
                )
                moved = (
                    stay * here
                    + rate_x * jnp.where(goes_east, west, east)
                    + rate_y * jnp.where(goes_north, south, north)
                )
                behind = jnp.where(first_direction, pltpu.roll(moved, 97, 1), pltpu.roll(moved, 1, 1))
                forward = jnp.where(last_direction, pltpu.roll(moved, 31, 1), pltpu.roll(moved, 127, 1))
                beside = jnp.where(turn_sign[rows, :] > 0.0, behind, forward)
                rate = turn_size[rows, :] * gain
                turned[rows, lanes] = (moved + rate * (beside - moved)) * sea[rows, :]

        for ahead in range(1, sections):
            pair_copy(step, ahead, True).wait_recv()

        message = arrived[step].reshape(CELLS, 128)
        high = round_half(message)
        pieces = jnp.where(low_half, pltpu.roll(high, 64, 1), message - high).astype(bf16)
        seen = jnp.dot(place_back, pieces, preferred_element_type=f32).astype(bf16)
        seen = jnp.concatenate([seen, seen[:, 0:64]], axis=1)
        drift = None
        for chunk in range(SPEC // 256):
            lanes = slice(256 * chunk, 256 * (chunk + 1))
            grow = jnp.dot(seen, swell_table[:, lanes], preferred_element_type=f32)
            waves = turned[:, lanes] * (1.0 + grow)
            if last:
                spectra_out[:, lanes] = waves
            else:
                state[step + 1, :, lanes] = waves
                part = stokes_part(waves, chunk)
                drift = part if drift is None else drift + part

        drag = jnp.where(low_half, message, pltpu.roll(message, 64, 1))
        for y in range(ROWS):
            rows = slice(COLS * y, COLS * (y + 1))
            lanes = slice(SPEC, WIDE)
            here = state[step, rows, lanes]
            west = jnp.where(first_column, west_halo[step, y : y + 1, lanes], pltpu.roll(here, 1, 0))
            east = jnp.where(last_column, east_halo[step, y : y + 1, lanes], pltpu.roll(here, COLS - 1, 0))
            south = state[step, COLS * (y - 1) : COLS * y, lanes] if y else south_halo[step, :, lanes]
            north = (
                state[step, COLS * (y + 1) : COLS * (y + 2), lanes] if y < ROWS - 1 else north_halo[step, :, lanes]
            )
            sheared = jnp.where(zonal, south - north, east - west)
            spin = 0.5 * (sheared + pltpu.roll(sheared, 32, 1))
            spin = spin + (0.2 + 0.6 * (global_row + y) / (ROWS * bands))
            pushed = pltpu.roll(here + drag[rows, :], 32, 1)
            flow = (keep * sea[rows, :]) * (here + twist * spin * pushed)
            if last:
                currents_out[rows, :] = flow[:, 0 : 2 * NDEPTH]
            else:
                state[step + 1, rows, lanes] = flow

        if not last:
            edge_rows(step + 1)
            each_halo(step + 1, lambda copy: copy.start())
            pack(step + 1, drift)
            send_pairs(step + 1)

    for step in range(STEPS):
        each_halo(step, lambda copy: copy.wait_send())
        for ahead in range(1, sections):
            pair_copy(step, ahead, False).wait_send()


def solution(mesh):
    sections, bands = mesh.shape["sec"], mesh.shape["lat"]
    rates, stokes_table, swell_table = build_tables()
    share = CELLS // sections

    def per_device(spectra, turning, currents, drag_rates, land_mask, ocean_target):
        f32, bf16 = jnp.float32, jnp.bfloat16
        vmem = pl.BlockSpec(memory_space=pltpu.VMEM)
        hbm = pl.BlockSpec(memory_space=pltpu.HBM)
        waves, flows = pl.pallas_call(
            lambda *refs: kernel(sections, bands, *refs),
            out_shape=(
                jax.ShapeDtypeStruct((CELLS, SPEC), f32),
                jax.ShapeDtypeStruct((CELLS, 2 * NDEPTH), f32),
            ),
            in_specs=[hbm, vmem, vmem, vmem, vmem, vmem, vmem, hbm, hbm],
            out_specs=(vmem, vmem),
            scratch_shapes=[
                pltpu.VMEM((STEPS, CELLS, WIDE), f32),
                pltpu.VMEM((STEPS, COLS, WIDE), f32),
                pltpu.VMEM((STEPS, COLS, WIDE), f32),
                pltpu.VMEM((STEPS, ROWS, WIDE), f32),
                pltpu.VMEM((STEPS, ROWS, WIDE), f32),
                pltpu.VMEM((STEPS, ROWS, WIDE), f32),
                pltpu.VMEM((STEPS, ROWS, WIDE), f32),
                pltpu.VMEM((STEPS, sections, share, 128), f32),
                pltpu.VMEM((STEPS, sections, share, 128), f32),
                pltpu.VMEM((CELLS, SPEC), f32),
                pltpu.VMEM((SPEC, 128), bf16),
                pltpu.VMEM((6 * NDEPTH, SPEC), bf16),
                pltpu.VMEM((4, 8, 128), f32),
                pltpu.VMEM((CELLS, 128), f32),
                pltpu.VMEM((CELLS, 128), f32),
                pltpu.VMEM((CELLS, 128), f32),
                pltpu.SemaphoreType.DMA((3,)),
                pltpu.SemaphoreType.DMA((STEPS, 2)),
                pltpu.SemaphoreType.DMA((STEPS, 2)),
                pltpu.SemaphoreType.DMA((STEPS, 2)),
                pltpu.SemaphoreType.DMA((STEPS, 2)),
                pltpu.SemaphoreType.DMA((STEPS, sections)),
                pltpu.SemaphoreType.DMA((STEPS, sections)),
            ],
            compiler_params=pltpu.CompilerParams(
                collective_id=0, has_side_effects=True, vmem_limit_bytes=24 << 20
            ),
        )(
            spectra.reshape(CELLS, SPEC),
            turning,
            currents,
            drag_rates.reshape(1, NDEPTH),
            land_mask,
            ocean_target,
            jnp.asarray(rates),
            jnp.asarray(stokes_table),
            jnp.asarray(swell_table),
        )
        return waves.reshape(ROWS, COLS, SPEC), flows.reshape(ROWS, COLS, 2 * NDEPTH)

    return jax.shard_map(
        per_device,
        mesh=mesh,
        in_specs=(
            P("lat", "sec", None),
            P("lat", "sec"),
            P("lat", "sec", None),
            P(),
            P("lat", "sec"),
            P("lat", "sec"),
        ),
        out_specs=(P("lat", "sec", None), P("lat", "sec", None)),
        check_vma=False,
    )
```

```python
import math

import jax
import jax.numpy as jnp
import ml_dtypes
import numpy as np
from jax import lax
from jax.experimental import pallas as pl
from jax.experimental.pallas import tpu as pltpu
from jax.sharding import PartitionSpec as P

NFREQ = 24
NDIR = 32
NDEPTH = 32
STEPS = 3
ROWS = 4
COLS = 24
CELLS = ROWS * COLS
SPEC = NFREQ * NDIR
WIDE = SPEC + 128

STOKES_SCALE = 0.1
OCEAN_DT = 0.3
CURRENT_GAIN = 0.2

MESH = pl.DeviceIdType.MESH


def halves(table):
    high = table.astype(ml_dtypes.bfloat16)
    low = (table - high.astype(np.float32)).astype(ml_dtypes.bfloat16)
    return high, low


def build_tables():
    f32 = np.float32
    fraction = np.arange(NFREQ, dtype=f32) / f32(NFREQ - 1)
    angles = (np.arange(NDIR, dtype=f32) + f32(0.5)) * f32(2.0 * math.pi / NDIR)
    east = np.cos(angles).astype(f32)
    north = np.sin(angles).astype(f32)
    compass = np.stack([east, north])
    courant = f32(0.1) + f32(0.3) * fraction
    depth_level = f32(0.5) + f32(NDEPTH - 2) * (f32(1.0) - fraction)
    levels = np.arange(NDEPTH, dtype=f32)
    weights = np.maximum(f32(1.0) - np.abs(levels[None, :] - depth_level[:, None]), f32(0.0))
    mean_weights = weights / np.sum(weights, axis=1, keepdims=True)
    x_rate = (courant[:, None] * east[None, :]).reshape(-1)
    y_rate = (courant[:, None] * north[None, :]).reshape(-1)
    turn_gain = f32(1.0) - f32(0.5) * fraction
    growth = f32(CURRENT_GAIN) * (f32(1.0) + fraction)
    stokes = (
        f32(STOKES_SCALE) * weights[:, None, None, :] * compass.T[None, :, :, None]
    ).reshape(SPEC, 2 * NDEPTH)
    swell = (
        growth[None, None, :, None] * mean_weights.T[None, :, :, None] * compass[:, None, None, :]
    ).reshape(2 * NDEPTH, SPEC)
    rates = np.zeros((8, SPEC), f32)
    rates[0] = f32(1.0) - np.abs(x_rate) - np.abs(y_rate)
    rates[1] = np.abs(x_rate)
    rates[2] = np.abs(y_rate)
    rates[3] = np.repeat(turn_gain, NDIR)
    stokes_table = np.concatenate(halves(stokes), axis=1)
    swell_high, swell_low = halves(swell)
    swell_table = np.concatenate([swell_high, swell_high, swell_low], axis=0)
    return rates, stokes_table, swell_table


def iota(shape, dim):
    return lax.broadcasted_iota(jnp.int32, shape, dim)


def round_half(x):
    return x.astype(jnp.bfloat16).astype(jnp.float32)


def kernel(
    sections,
    bands,
    spectra_hbm,
    turning_hbm,
    currents_hbm,
    drag_hbm,
    land_hbm,
    target_hbm,
    rates_hbm,
    stokes_hbm,
    swell_hbm,
    spectra_out,
    currents_out,
    waves,
    flows,
    wave_south,
    wave_north,
    wave_west,
    wave_east,
    flow_south,
    flow_north,
    flow_west,
    flow_east,
    wave_edges,
    flow_edges,
    outgoing,
    arrived,
    turned,
    spins,
    drifts,
    flow_at_waves,
    turning_ref,
    currents_ref,
    drag_ref,
    land_ref,
    target_ref,
    rates_ref,
    stokes_table,
    swell_table,
    tiny,
    turn_size,
    turn_sign,
    sea,
    load_sem,
    halo_send,
    halo_recv,
    pair_send,
    pair_recv,
):
    f32, bf16 = jnp.float32, jnp.bfloat16
    share = CELLS // sections
    sec = lax.axis_index("sec")
    lat = lax.axis_index("lat")
    has_west, has_east = sec > 0, sec < sections - 1
    has_south, has_north = lat > 0, lat < bands - 1

    barrier = pltpu.get_barrier_semaphore()
    for ahead in range(1, sections):
        peer = lax.rem(sec + ahead, sections)
        pl.semaphore_signal(barrier, inc=1, device_id={"sec": peer}, device_id_type=MESH)

    @pl.when(has_south)
    def _():
        pl.semaphore_signal(barrier, inc=1, device_id={"lat": lat - 1}, device_id_type=MESH)

    @pl.when(has_north)
    def _():
        pl.semaphore_signal(barrier, inc=1, device_id={"lat": lat + 1}, device_id_type=MESH)

    pairs = (
        (turning_hbm, turning_ref),
        (drag_hbm, drag_ref),
        (land_hbm, land_ref),
        (target_hbm, target_ref),
        (currents_hbm, currents_ref),
        (rates_hbm, rates_ref),
        (spectra_hbm, waves.at[0]),
        (stokes_hbm, stokes_table),
        (swell_hbm, swell_table),
    )
    loads = [pltpu.make_async_copy(there, here, load_sem.at[i]) for i, (there, here) in enumerate(pairs)]
    for load in loads:
        load.start()

    for there, halos in (
        (has_south, (wave_south, flow_south)),
        (has_north, (wave_north, flow_north)),
        (has_west, (wave_west, flow_west)),
        (has_east, (wave_east, flow_east)),
    ):

        @pl.when(jnp.logical_not(there))
        def _():
            for halo in halos:
                halo[...] = jnp.zeros_like(halo)

    tiny[...] = jnp.zeros_like(tiny)
    for load in loads[:4]:
        load.wait()
    tiny[0, 0:ROWS, 0:COLS] = turning_ref[...]
    tiny[1, 0:ROWS, 0:COLS] = land_ref[...].astype(f32)
    tiny[2, 0:ROWS, 0:COLS] = target_ref[...].astype(f32)
    tiny[3, 0:1, 0:NDEPTH] = 1.0 - drag_ref[...]

    lane_row = iota((1, 128), 1)
    target_rows = tiny[2]
    targets = jnp.full((1, 128), 99.0, f32)
    for y in range(ROWS):
        row = target_rows[y : y + 1, :]
        moved = pltpu.roll(row, COLS * y, 1) if y else row
        inside = jnp.logical_and(lane_row >= COLS * y, lane_row < COLS * (y + 1))
        targets = jnp.where(inside, moved, targets)
    matches = (iota((16, 128), 0).astype(f32) == targets).astype(f32)
    earlier = (iota((128, 128), 0) < iota((128, 128), 1)).astype(f32)
    before = jnp.dot(matches.astype(bf16), earlier.astype(bf16), preferred_element_type=f32)
    rank = jnp.sum(matches * before, axis=0, keepdims=True)
    place_of = targets * share + rank
    place = (iota((128, 128), 0).astype(f32) == place_of).astype(f32)
    place_back = jnp.transpose(place)[0:CELLS, 0:CELLS].astype(bf16)
    place = place[0:CELLS, 0:CELLS].astype(bf16)

    turn_columns = jnp.transpose(tiny[0])
    sea_columns = jnp.transpose(tiny[1])
    for y in range(ROWS):
        rows = slice(COLS * y, COLS * (y + 1))
        turn = jnp.broadcast_to(turn_columns[0:COLS, y : y + 1], (COLS, 128))
        turn_size[rows, :] = jnp.abs(turn)
        turn_sign[rows, :] = turn
        sea[rows, :] = jnp.broadcast_to(sea_columns[0:COLS, y : y + 1], (COLS, 128))

    keep = tiny[3, 0:1, :]
    keep = keep + pltpu.roll(keep, 32, 1)
    keep = keep + pltpu.roll(keep, 64, 1)

    lane = iota((COLS, 128), 1)
    line = iota((COLS, 128), 0)
    first_column = line == 0
    last_column = line == COLS - 1
    direction = lane & (NDIR - 1)
    goes_east = jnp.logical_or(direction < NDIR // 4, direction >= 3 * NDIR // 4)
    goes_north = direction < NDIR // 2
    first_direction = direction == 0
    last_direction = direction == NDIR - 1
    full_lane = iota((CELLS, 128), 1)
    low_half = full_lane < 64
    zonal = (full_lane & 63) < 32
    zonal_row = (lane & 63) < 32
    twist = jnp.where(zonal, OCEAN_DT, -OCEAN_DT)
    global_row = (lat * ROWS).astype(f32)

    def halo_copies(step, is_flow):
        own = (flows if is_flow else waves).at[step]
        edges = (flow_edges if is_flow else wave_edges).at[step]
        south, north, west, east = (
            (flow_south, flow_north, flow_west, flow_east)
            if is_flow
            else (wave_south, wave_north, wave_west, wave_east)
        )
        index = 2 * step + is_flow
        plan = (
            (has_west, has_east, edges.at[0], east, {"sec": sec - 1}),
            (has_east, has_west, edges.at[1], west, {"sec": sec + 1}),
            (has_south, has_north, own.at[pl.ds(0, COLS)], north, {"lat": lat - 1}),
            (has_north, has_south, own.at[pl.ds(CELLS - COLS, COLS)], south, {"lat": lat + 1}),
        )
        for k, (sends, receives, source, halo, device) in enumerate(plan):
            copy = lambda source=source, halo=halo, device=device, k=k: pltpu.make_async_remote_copy(
                src_ref=source,
                dst_ref=halo.at[step],
                send_sem=halo_send.at[index, k],
                recv_sem=halo_recv.at[index, k],
                device_id=device,
                device_id_type=MESH,
            )
            yield sends, receives, copy

    def send_halos(step, is_flow):
        own, edges = (flows, flow_edges) if is_flow else (waves, wave_edges)
        for y in range(ROWS):
            edges[step, 0, y : y + 1, :] = own[step, COLS * y : COLS * y + 1, :]
            edges[step, 1, y : y + 1, :] = own[step, COLS * (y + 1) - 1 : COLS * (y + 1), :]
        for sends, _, copy in halo_copies(step, is_flow):

            @pl.when(sends)
            def _():
                copy().start()

    def receive_halos(step, is_flow):
        for _, receives, copy in halo_copies(step, is_flow):

            @pl.when(receives)
            def _():
                copy().wait_recv()

    def pair_copy(index, ahead, source):
        peer = lax.rem(sec + ahead, sections)
        slot = lax.rem(sec + sections - ahead, sections) if source else sec
        return pltpu.make_async_remote_copy(
            src_ref=outgoing.at[index, peer],
            dst_ref=arrived.at[index, slot],
            send_sem=pair_send.at[index, ahead],
            recv_sem=pair_recv.at[index, slot],
            device_id={"sec": peer},
            device_id_type=MESH,
        )

    def send_pairs(index, message):
        outgoing[index] = message.reshape(sections, share, 128)
        for ahead in range(1, sections):
            pair_copy(index, ahead, False).start()
        arrived[index, sec] = outgoing[index, sec]

    def receive_pairs(index):
        for ahead in range(1, sections):
            pair_copy(index, ahead, True).wait_recv()
        return arrived[index].reshape(CELLS, 128)

    def stokes_part(values, chunk):
        high = values.astype(bf16)
        low = (values - high.astype(f32)).astype(bf16)
        both = jnp.concatenate([high, low], axis=0)
        return jnp.dot(both, stokes_table[256 * chunk : 256 * (chunk + 1), :], preferred_element_type=f32)

    def sorted_drift(step, drift):
        drift = drift[0:CELLS] + drift[CELLS:]
        drift = drift + pltpu.roll(drift, 64, 1)
        drifts[step] = drift
        high = round_half(drift)
        pieces = jnp.where(low_half, high, drift - high).astype(bf16)
        drift = jnp.dot(place, pieces, preferred_element_type=f32)
        return drift + pltpu.roll(drift, 64, 1)

    def neighbours(own, halos, step, y, lanes):
        south, north, west, east = halos
        rows = slice(COLS * y, COLS * (y + 1))
        here = own[step, rows, lanes]
        return (
            here,
            jnp.where(first_column, west[step, y : y + 1, lanes], pltpu.roll(here, 1, 0)),
            jnp.where(last_column, east[step, y : y + 1, lanes], pltpu.roll(here, COLS - 1, 0)),
            own[step, COLS * (y - 1) : COLS * y, lanes] if y else south[step, :, lanes],
            own[step, COLS * (y + 1) : COLS * (y + 2), lanes] if y < ROWS - 1 else north[step, :, lanes],
        )

    def find_spin(step):
        for y in range(ROWS):
            _, west, east, south, north = neighbours(
                flows, (flow_south, flow_north, flow_west, flow_east), step, y, slice(0, 128)
            )
            sheared = jnp.where(zonal_row, south - north, east - west)
            spin = 0.5 * (sheared + pltpu.roll(sheared, 32, 1))
            spins[step, COLS * y : COLS * (y + 1), :] = spin + (0.2 + 0.6 * (global_row + y) / (ROWS * bands))

    def advect(step):
        for chunk in range(SPEC // 128):
            lanes = slice(128 * chunk, 128 * (chunk + 1))
            stay = rates_ref[0:1, lanes]
            rate_x = rates_ref[1:2, lanes]
            rate_y = rates_ref[2:3, lanes]
            gain = rates_ref[3:4, lanes]
            for y in range(ROWS):
                rows = slice(COLS * y, COLS * (y + 1))
                here, west, east, south, north = neighbours(
                    waves, (wave_south, wave_north, wave_west, wave_east), step, y, lanes
                )
                moved = (
                    stay * here
                    + rate_x * jnp.where(goes_east, west, east)
                    + rate_y * jnp.where(goes_north, south, north)
                )
                behind = jnp.where(first_direction, pltpu.roll(moved, 97, 1), pltpu.roll(moved, 1, 1))
                forward = jnp.where(last_direction, pltpu.roll(moved, 31, 1), pltpu.roll(moved, 127, 1))
                beside = jnp.where(turn_sign[rows, :] > 0.0, behind, forward)
                rate = turn_size[rows, :] * gain
                turned[rows, lanes] = (moved + rate * (beside - moved)) * sea[rows, :]

    def push(flow, spin, drift, wet):
        return (keep * wet) * (flow + twist * spin * pltpu.roll(flow + drift, 32, 1))

    def grow(seen, step):
        seen = jnp.concatenate([seen, seen[:, 0:64]], axis=1)
        drift = None
        for chunk in range(SPEC // 256):
            lanes = slice(256 * chunk, 256 * (chunk + 1))
            growth = jnp.dot(seen, swell_table[:, lanes], preferred_element_type=f32)
            values = turned[:, lanes] * (1.0 + growth)
            if step == STEPS:
                spectra_out[:, lanes] = values
            else:
                waves[step, :, lanes] = values
        if step == STEPS:
            return None
        send_halos(step, 0)
        return find_drift(step)

    def find_drift(step):
        drift = None
        for chunk in range(SPEC // 256):
            part = stokes_part(waves[step, :, 256 * chunk : 256 * (chunk + 1)], chunk)
            drift = part if drift is None else drift + part
        return sorted_drift(step, drift)

    def first_seen(message):
        high = round_half(message)
        pieces = jnp.where(low_half, pltpu.roll(high, 64, 1), message - high).astype(bf16)
        seen = jnp.dot(place_back, pieces, preferred_element_type=f32)
        flow_at_waves[0] = seen + pltpu.roll(seen, 64, 1)
        return seen.astype(bf16)

    def next_seen(step, message):
        high = round_half(message)
        pieces = jnp.where(low_half, high, message - high).astype(bf16)
        both = jnp.dot(place_back, pieces, preferred_element_type=f32)
        both = both + pltpu.roll(both, 64, 1)
        other = pltpu.roll(both, 32, 1)
        spin = jnp.where(zonal, both, other)
        wet = jnp.where(zonal, other, both)
        flow = push(flow_at_waves[step - 1], spin, drifts[step - 1], wet)
        flow_at_waves[step] = flow
        high = round_half(flow)
        return jnp.where(low_half, high, flow - high).astype(bf16)

    def spin_message(step):
        return jnp.where(zonal, spins[step], sea[...])

    loads[4].wait()
    start_flow = currents_ref[...].reshape(CELLS, 2 * NDEPTH)
    flows[0] = jnp.concatenate([start_flow, start_flow], axis=1)
    for load in loads[5:]:
        load.wait()
    drift = find_drift(0)

    greeted = sections - 1 + has_south.astype(jnp.int32) + has_north.astype(jnp.int32)
    pl.semaphore_wait(barrier, greeted)

    send_halos(0, 1)
    send_pairs(0, jnp.where(low_half, drift, flows[0]))
    send_halos(0, 0)

    receive_halos(0, 1)
    find_spin(0)
    send_pairs(1, spin_message(0))
    receive_halos(0, 0)
    advect(0)
    message = receive_pairs(0)
    flows[1] = push(flows[0], spins[0], jnp.where(low_half, message, pltpu.roll(message, 64, 1)), sea[...])
    send_halos(1, 1)
    send_pairs(2, grow(first_seen(message), 1))

    receive_halos(1, 1)
    find_spin(1)
    send_pairs(3, spin_message(1))
    receive_halos(1, 0)
    advect(1)
    send_pairs(4, grow(next_seen(1, receive_pairs(1)), 2))
    flows[2] = push(flows[1], spins[1], receive_pairs(2), sea[...])
    send_halos(2, 1)

    receive_halos(2, 0)
    advect(2)
    grow(next_seen(2, receive_pairs(3)), 3)
    receive_halos(2, 1)
    find_spin(2)
    currents_out[...] = push(flows[2], spins[2], receive_pairs(4), sea[...])[:, 0 : 2 * NDEPTH]

    for step in range(STEPS):
        for is_flow in (0, 1):
            for sends, _, copy in halo_copies(step, is_flow):

                @pl.when(sends)
                def _():
                    copy().wait_send()

    for index in range(2 * STEPS - 1):
        for ahead in range(1, sections):
            pair_copy(index, ahead, False).wait_send()


def store(waves_ref, flows_ref, waves_out, flows_out, sems):
    copies = [
        pltpu.make_async_copy(waves_ref, waves_out, sems.at[0]),
        pltpu.make_async_copy(flows_ref, flows_out, sems.at[1]),
    ]
    for copy in copies:
        copy.start()
    for copy in copies:
        copy.wait()


def solution(mesh):
    sections, bands = mesh.shape["sec"], mesh.shape["lat"]
    rates, stokes_table, swell_table = build_tables()
    share = CELLS // sections

    def per_device(spectra, turning, currents, drag_rates, land_mask, ocean_target):
        f32, bf16 = jnp.float32, jnp.bfloat16
        vmem = pl.BlockSpec(memory_space=pltpu.VMEM)
        hbm = pl.BlockSpec(memory_space=pltpu.HBM)
        operands = (
            spectra.reshape(CELLS, SPEC),
            turning,
            currents,
            drag_rates.reshape(1, NDEPTH),
            land_mask,
            ocean_target,
            jnp.asarray(rates),
            jnp.asarray(stokes_table),
            jnp.asarray(swell_table),
        )
        waves, flows = pl.pallas_call(
            lambda *refs: kernel(sections, bands, *refs),
            out_shape=(
                jax.ShapeDtypeStruct((CELLS, SPEC), f32),
                jax.ShapeDtypeStruct((CELLS, 2 * NDEPTH), f32),
            ),
            in_specs=[hbm] * 9,
            out_specs=(vmem, vmem),
            scratch_shapes=[
                pltpu.VMEM((STEPS, CELLS, SPEC), f32),
                pltpu.VMEM((STEPS, CELLS, 128), f32),
                pltpu.VMEM((STEPS, COLS, SPEC), f32),
                pltpu.VMEM((STEPS, COLS, SPEC), f32),
                pltpu.VMEM((STEPS, ROWS, SPEC), f32),
                pltpu.VMEM((STEPS, ROWS, SPEC), f32),
                pltpu.VMEM((STEPS, COLS, 128), f32),
                pltpu.VMEM((STEPS, COLS, 128), f32),
                pltpu.VMEM((STEPS, ROWS, 128), f32),
                pltpu.VMEM((STEPS, ROWS, 128), f32),
                pltpu.VMEM((STEPS, 2, ROWS, SPEC), f32),
                pltpu.VMEM((STEPS, 2, ROWS, 128), f32),
                pltpu.VMEM((2 * STEPS - 1, sections, share, 128), f32),
                pltpu.VMEM((2 * STEPS - 1, sections, share, 128), f32),
                pltpu.VMEM((CELLS, SPEC), f32),
                pltpu.VMEM((STEPS, CELLS, 128), f32),
                pltpu.VMEM((STEPS, CELLS, 128), f32),
                pltpu.VMEM((STEPS, CELLS, 128), f32),
                pltpu.VMEM((ROWS, COLS), f32),
                pltpu.VMEM((ROWS, COLS, 2 * NDEPTH), f32),
                pltpu.VMEM((1, NDEPTH), f32),
                pltpu.VMEM((ROWS, COLS), jnp.int32),
                pltpu.VMEM((ROWS, COLS), jnp.int32),
                pltpu.VMEM((8, SPEC), f32),
                pltpu.VMEM((SPEC, 128), bf16),
                pltpu.VMEM((6 * NDEPTH, SPEC), bf16),
                pltpu.VMEM((4, 8, 128), f32),
                pltpu.VMEM((CELLS, 128), f32),
                pltpu.VMEM((CELLS, 128), f32),
                pltpu.VMEM((CELLS, 128), f32),
                pltpu.SemaphoreType.DMA((9,)),
                pltpu.SemaphoreType.DMA((2 * STEPS, 4)),
                pltpu.SemaphoreType.DMA((2 * STEPS, 4)),
                pltpu.SemaphoreType.DMA((2 * STEPS - 1, sections)),
                pltpu.SemaphoreType.DMA((2 * STEPS - 1, sections)),
            ],
            compiler_params=pltpu.CompilerParams(
                collective_id=0, has_side_effects=True, vmem_limit_bytes=24 << 20
            ),
        )(*[pltpu.with_memory_space_constraint(x, pltpu.HBM) for x in operands])
        waves, flows = pl.pallas_call(
            store,
            out_shape=(
                jax.ShapeDtypeStruct((CELLS, SPEC), f32),
                jax.ShapeDtypeStruct((CELLS, 2 * NDEPTH), f32),
            ),
            in_specs=[vmem, vmem],
            out_specs=(hbm, hbm),
            scratch_shapes=[pltpu.SemaphoreType.DMA((2,))],
        )(*[pltpu.with_memory_space_constraint(x, pltpu.VMEM) for x in (waves, flows)])
        return waves.reshape(ROWS, COLS, SPEC), flows.reshape(ROWS, COLS, 2 * NDEPTH)

    return jax.shard_map(
        per_device,
        mesh=mesh,
        in_specs=(
            P("lat", "sec", None),
            P("lat", "sec"),
            P("lat", "sec", None),
            P(),
            P("lat", "sec"),
            P("lat", "sec"),
        ),
        out_specs=(P("lat", "sec", None), P("lat", "sec", None)),
        check_vma=False,
    )
```

```python
import math

import jax
import jax.numpy as jnp
import ml_dtypes
import numpy as np
from jax import lax
from jax.experimental import pallas as pl
from jax.experimental.pallas import tpu as pltpu
from jax.sharding import PartitionSpec as P

NFREQ = 24
NDIR = 32
NDEPTH = 32
STEPS = 3
ROWS = 4
COLS = 24
CELLS = ROWS * COLS
SPEC = NFREQ * NDIR
RING = 3

STOKES_SCALE = 0.1
OCEAN_DT = 0.3
CURRENT_GAIN = 0.2

MESH = pl.DeviceIdType.MESH


def halves(table):
    high = table.astype(ml_dtypes.bfloat16)
    low = (table - high.astype(np.float32)).astype(ml_dtypes.bfloat16)
    return high, low


def build_tables():
    f32 = np.float32
    fraction = np.arange(NFREQ, dtype=f32) / f32(NFREQ - 1)
    angles = (np.arange(NDIR, dtype=f32) + f32(0.5)) * f32(2.0 * math.pi / NDIR)
    east = np.cos(angles).astype(f32)
    north = np.sin(angles).astype(f32)
    compass = np.stack([east, north])
    courant = f32(0.1) + f32(0.3) * fraction
    depth_level = f32(0.5) + f32(NDEPTH - 2) * (f32(1.0) - fraction)
    levels = np.arange(NDEPTH, dtype=f32)
    weights = np.maximum(f32(1.0) - np.abs(levels[None, :] - depth_level[:, None]), f32(0.0))
    mean_weights = weights / np.sum(weights, axis=1, keepdims=True)
    x_rate = (courant[:, None] * east[None, :]).reshape(-1)
    y_rate = (courant[:, None] * north[None, :]).reshape(-1)
    turn_gain = f32(1.0) - f32(0.5) * fraction
    growth = f32(CURRENT_GAIN) * (f32(1.0) + fraction)
    stokes = (
        f32(STOKES_SCALE) * weights[:, None, None, :] * compass.T[None, :, :, None]
    ).reshape(SPEC, 2 * NDEPTH)
    swell = (
        growth[None, None, :, None] * mean_weights.T[None, :, :, None] * compass[:, None, None, :]
    ).reshape(2 * NDEPTH, SPEC)
    rates = np.zeros((8, SPEC), f32)
    rates[0] = f32(1.0) - np.abs(x_rate) - np.abs(y_rate)
    rates[1] = np.abs(x_rate)
    rates[2] = np.abs(y_rate)
    rates[3] = np.repeat(turn_gain, NDIR)
    stokes_table = np.concatenate(halves(stokes), axis=1)
    swell_high, swell_low = halves(swell)
    swell_table = np.concatenate([swell_high, swell_high, swell_low], axis=0)
    return rates, stokes_table, swell_table


def iota(shape, dim):
    return lax.broadcasted_iota(jnp.int32, shape, dim)


def round_half(x):
    return x.astype(jnp.bfloat16).astype(jnp.float32)


def kernel(
    sections,
    bands,
    spectra_hbm,
    turning_hbm,
    currents_hbm,
    drag_hbm,
    land_hbm,
    target_hbm,
    rates_hbm,
    stokes_hbm,
    swell_hbm,
    spectra_out,
    currents_out,
    waves,
    flows,
    wave_south,
    wave_north,
    wave_west,
    wave_east,
    flow_south,
    flow_north,
    flow_west,
    flow_east,
    wave_edges,
    flow_edges,
    outgoing,
    arrived,
    half_out,
    half_in,
    unpacked,
    edge_lines,
    band_edges,
    turned,
    growths,
    spins,
    drifts,
    flow_at_waves,
    turning_ref,
    currents_ref,
    drag_ref,
    land_ref,
    target_ref,
    rates_ref,
    stokes_table,
    swell_table,
    tiny,
    turn_size,
    turn_sign,
    sea,
    load_sem,
    halo_send,
    halo_recv,
    pair_send,
    pair_recv,
):
    f32, bf16 = jnp.float32, jnp.bfloat16
    share = CELLS // sections
    sec = lax.axis_index("sec")
    lat = lax.axis_index("lat")
    has_west, has_east = sec > 0, sec < sections - 1
    has_south, has_north = lat > 0, lat < bands - 1

    lines = sections // RING
    line, spot = lax.div(sec, RING), lax.rem(sec, RING)
    hops = sorted(
        ((over, along) for over in range(lines) for along in range(RING) if over or along),
        key=lambda hop: (hop[1] == 0, -min(hop[0], lines - hop[0])),
    )

    def peer_of(hop):
        return RING * lax.rem(line + hop[0], lines) + lax.rem(spot + hop[1], RING)

    def source_of(hop):
        return RING * lax.rem(line + lines - hop[0], lines) + lax.rem(spot + RING - hop[1], RING)

    barrier = pltpu.get_barrier_semaphore()
    for hop in hops:
        peer = peer_of(hop)
        pl.semaphore_signal(barrier, inc=1, device_id={"sec": peer}, device_id_type=MESH)

    @pl.when(has_south)
    def _():
        pl.semaphore_signal(barrier, inc=1, device_id={"lat": lat - 1}, device_id_type=MESH)

    @pl.when(has_north)
    def _():
        pl.semaphore_signal(barrier, inc=1, device_id={"lat": lat + 1}, device_id_type=MESH)

    pairs = (
        (turning_hbm, turning_ref),
        (drag_hbm, drag_ref),
        (land_hbm, land_ref),
        (target_hbm, target_ref),
        (currents_hbm, currents_ref),
        (rates_hbm, rates_ref),
        (spectra_hbm, waves.at[0]),
        (stokes_hbm, stokes_table),
        (swell_hbm, swell_table),
    )
    loads = [pltpu.make_async_copy(there, here, load_sem.at[i]) for i, (there, here) in enumerate(pairs)]
    for load in loads:
        load.start()

    for there, halos in (
        (has_south, (wave_south, flow_south)),
        (has_north, (wave_north, flow_north)),
        (has_west, (wave_west, flow_west)),
        (has_east, (wave_east, flow_east)),
    ):

        @pl.when(jnp.logical_not(there))
        def _():
            for halo in halos:
                halo[...] = jnp.zeros_like(halo)

    tiny[...] = jnp.zeros_like(tiny)
    for load in loads[:4]:
        load.wait()
    tiny[0, 0:ROWS, 0:COLS] = turning_ref[...]
    tiny[1, 0:ROWS, 0:COLS] = land_ref[...].astype(f32)
    tiny[2, 0:ROWS, 0:COLS] = target_ref[...].astype(f32)
    tiny[3, 0:1, 0:NDEPTH] = 1.0 - drag_ref[...]

    lane_row = iota((1, 128), 1)
    target_rows = tiny[2]
    targets = jnp.full((1, 128), 99.0, f32)
    for y in range(ROWS):
        row = target_rows[y : y + 1, :]
        moved = pltpu.roll(row, COLS * y, 1) if y else row
        inside = jnp.logical_and(lane_row >= COLS * y, lane_row < COLS * (y + 1))
        targets = jnp.where(inside, moved, targets)
    matches = (iota((16, 128), 0).astype(f32) == targets).astype(f32)
    earlier = (iota((128, 128), 0) < iota((128, 128), 1)).astype(f32)
    before = jnp.dot(matches.astype(bf16), earlier.astype(bf16), preferred_element_type=f32)
    rank = jnp.sum(matches * before, axis=0, keepdims=True)
    place_of = targets * share + rank
    place = (iota((128, 128), 0).astype(f32) == place_of).astype(f32)
    place_back = jnp.transpose(place)[0:CELLS, 0:CELLS].astype(bf16)
    place = place[0:CELLS, 0:CELLS].astype(bf16)

    turn_columns = jnp.transpose(tiny[0])
    sea_columns = jnp.transpose(tiny[1])
    for y in range(ROWS):
        rows = slice(COLS * y, COLS * (y + 1))
        turn = jnp.broadcast_to(turn_columns[0:COLS, y : y + 1], (COLS, 128))
        turn_size[rows, :] = jnp.abs(turn)
        turn_sign[rows, :] = turn
        sea[rows, :] = jnp.broadcast_to(sea_columns[0:COLS, y : y + 1], (COLS, 128))

    keep = tiny[3, 0:1, :]
    keep = keep + pltpu.roll(keep, 32, 1)
    keep = keep + pltpu.roll(keep, 64, 1)

    lane = iota((COLS, 128), 1)
    column = iota((COLS, 128), 0)
    first_column = column == 0
    last_column = column == COLS - 1
    direction = lane & (NDIR - 1)
    goes_east = jnp.logical_or(direction < NDIR // 4, direction >= 3 * NDIR // 4)
    goes_north = direction < NDIR // 2
    first_direction = direction == 0
    last_direction = direction == NDIR - 1
    full_lane = iota((CELLS, 128), 1)
    low_half = full_lane < 64
    zonal = (full_lane & 63) < 32
    low_rows = iota((share // 2, 128), 1) < 64
    zonal_row = (lane & 63) < 32
    twist = jnp.where(zonal, OCEAN_DT, -OCEAN_DT)
    global_row = (lat * ROWS).astype(f32)

    def halo_copies(step, is_flow):
        edges = (flow_edges if is_flow else wave_edges).at[step]
        if is_flow:
            first = flows.at[step, pl.ds(0, COLS)]
            final = flows.at[step, pl.ds(CELLS - COLS, COLS)]
        else:
            first, final = band_edges.at[step, 0], band_edges.at[step, 1]
        south, north, west, east = (
            (flow_south, flow_north, flow_west, flow_east)
            if is_flow
            else (wave_south, wave_north, wave_west, wave_east)
        )
        index = 2 * step + is_flow
        plan = (
            (has_west, has_east, edges.at[0], east, {"sec": sec - 1}),
            (has_east, has_west, edges.at[1], west, {"sec": sec + 1}),
            (has_south, has_north, first, north, {"lat": lat - 1}),
            (has_north, has_south, final, south, {"lat": lat + 1}),
        )
        for k, (sends, receives, source, halo, device) in enumerate(plan):
            copy = lambda source=source, halo=halo, device=device, k=k: pltpu.make_async_remote_copy(
                src_ref=source,
                dst_ref=halo.at[step],
                send_sem=halo_send.at[index, k],
                recv_sem=halo_recv.at[index, k],
                device_id=device,
                device_id_type=MESH,
            )
            yield sends, receives, copy

    def pack(tiles, needed):
        return [
            jnp.where(needed[0 : tiles[0].shape[0]], tiles[2 * c], pltpu.roll(tiles[2 * c + 1], 16, 1))
            for c in range(SPEC // 256)
        ]

    def unpack(halo, chunk):
        return pltpu.roll(halo, 112, 1) if chunk % 2 else halo

    def half_lanes(chunk):
        return slice(128 * (chunk // 2), 128 * (chunk // 2 + 1))

    def tiles_of(values):
        return [values[:, 128 * c : 128 * (c + 1)] for c in range(SPEC // 128)]

    def send_halos(step, is_flow):
        if is_flow:
            for y in range(ROWS):
                flow_edges[step, 0, y : y + 1, :] = flows[step, COLS * y : COLS * y + 1, :]
                flow_edges[step, 1, y : y + 1, :] = flows[step, COLS * (y + 1) - 1 : COLS * (y + 1), :]
        else:
            for y in range(ROWS):
                edge_lines[0, y : y + 1, :] = waves[step, COLS * y : COLS * y + 1, :]
                edge_lines[1, y : y + 1, :] = waves[step, COLS * (y + 1) - 1 : COLS * (y + 1), :]
            places = (
                (wave_edges, 0, edge_lines[0], jnp.logical_not(goes_east)),
                (wave_edges, 1, edge_lines[1], goes_east),
                (band_edges, 0, waves[step, 0:COLS, :], jnp.logical_not(goes_north)),
                (band_edges, 1, waves[step, CELLS - COLS : CELLS, :], goes_north),
            )
            for edges, side, values, needed in places:
                for c, tile in enumerate(pack(tiles_of(values), needed)):
                    edges[step, side, :, 128 * c : 128 * (c + 1)] = tile
        for sends, _, copy in halo_copies(step, is_flow):

            @pl.when(sends)
            def _():
                copy().start()

    def receive_halos(step, is_flow):
        for _, receives, copy in halo_copies(step, is_flow):

            @pl.when(receives)
            def _():
                copy().wait_recv()

    def pair_copy(index, k, source):
        peer = peer_of(hops[k])
        slot = source_of(hops[k]) if source else sec
        return pltpu.make_async_remote_copy(
            src_ref=half_out.at[index - 1, peer] if index else outgoing.at[peer],
            dst_ref=half_in.at[index - 1, slot] if index else arrived.at[slot],
            send_sem=pair_send.at[index, k],
            recv_sem=pair_recv.at[index, slot],
            device_id={"sec": peer},
            device_id_type=MESH,
        )

    def start_pairs(index):
        for k in range(sections - 1):
            pair_copy(index, k, False).start()

    def send_first(message):
        outgoing[...] = message.reshape(sections, share, 128)
        start_pairs(0)
        arrived[sec] = outgoing[sec]

    def receive(index):
        for k in range(sections - 1):
            pair_copy(index, k, True).wait_recv()

    def receive_first():
        receive(0)
        return arrived[...].reshape(CELLS, 128)

    def send_pairs(index, message):
        folded = jnp.where(low_half, message, pltpu.roll(message, CELLS - share // 2, 0))
        for k in range(sections):
            half_out[index - 1, k] = folded[share * k : share * k + share // 2, :]
        start_pairs(index)
        half_in[index - 1, sec] = half_out[index - 1, sec]

    def receive_pairs(index):
        receive(index)
        for k in range(sections):
            rows = half_in[index - 1, k]
            other = pltpu.roll(rows, 64, 1)
            unpacked[index - 1, share * k : share * k + share // 2, :] = jnp.where(low_rows, rows, other)
            unpacked[index - 1, share * k + share // 2 : share * (k + 1), :] = jnp.where(low_rows, other, rows)
        return unpacked[index - 1]

    def sent_halos(step, is_flow):
        for sends, _, copy in halo_copies(step, is_flow):

            @pl.when(sends)
            def _():
                copy().wait_send()

    def sent_pairs(index):
        for k in range(sections - 1):
            pair_copy(index, k, False).wait_send()

    def stokes_part(values, chunk):
        high = values.astype(bf16)
        low = (values - high.astype(f32)).astype(bf16)
        both = jnp.concatenate([high, low], axis=0)
        return jnp.dot(both, stokes_table[256 * chunk : 256 * (chunk + 1), :], preferred_element_type=f32)

    def sorted_drift(step, drift):
        drift = drift[0:CELLS] + drift[CELLS:]
        drift = drift + pltpu.roll(drift, 64, 1)
        drifts[step] = drift
        high = round_half(drift)
        pieces = jnp.where(low_half, high, drift - high).astype(bf16)
        drift = jnp.dot(place, pieces, preferred_element_type=f32)
        return drift + pltpu.roll(drift, 64, 1)

    def neighbours(own, halos, step, y, lanes, chunk=None):
        south, north, west, east = halos
        rows = slice(COLS * y, COLS * (y + 1))
        here = own[step, rows, lanes]
        edge = lanes if chunk is None else half_lanes(chunk)
        fit = (lambda halo: halo) if chunk is None else (lambda halo: unpack(halo, chunk))
        return (
            here,
            jnp.where(first_column, fit(west[step, y : y + 1, edge]), pltpu.roll(here, 1, 0)),
            jnp.where(last_column, fit(east[step, y : y + 1, edge]), pltpu.roll(here, COLS - 1, 0)),
            own[step, COLS * (y - 1) : COLS * y, lanes] if y else fit(south[step, :, edge]),
            own[step, COLS * (y + 1) : COLS * (y + 2), lanes] if y < ROWS - 1 else fit(north[step, :, edge]),
        )

    def find_spin(step):
        for y in range(ROWS):
            _, west, east, south, north = neighbours(
                flows, (flow_south, flow_north, flow_west, flow_east), step, y, slice(0, 128)
            )
            sheared = jnp.where(zonal_row, south - north, east - west)
            spin = 0.5 * (sheared + pltpu.roll(sheared, 32, 1))
            spins[step, COLS * y : COLS * (y + 1), :] = spin + (0.2 + 0.6 * (global_row + y) / (ROWS * bands))

    def advect(step, grown=False):
        drift = None
        for chunk in range(SPEC // 128):
            lanes = slice(128 * chunk, 128 * (chunk + 1))
            stay = rates_ref[0:1, lanes]
            rate_x = rates_ref[1:2, lanes]
            rate_y = rates_ref[2:3, lanes]
            gain = rates_ref[3:4, lanes]
            for y in range(ROWS):
                rows = slice(COLS * y, COLS * (y + 1))
                here, west, east, south, north = neighbours(
                    waves, (wave_south, wave_north, wave_west, wave_east), step, y, lanes, chunk
                )
                moved = (
                    stay * here
                    + rate_x * jnp.where(goes_east, west, east)
                    + rate_y * jnp.where(goes_north, south, north)
                )
                behind = jnp.where(first_direction, pltpu.roll(moved, 97, 1), pltpu.roll(moved, 1, 1))
                forward = jnp.where(last_direction, pltpu.roll(moved, 31, 1), pltpu.roll(moved, 127, 1))
                beside = jnp.where(turn_sign[rows, :] > 0.0, behind, forward)
                rate = turn_size[rows, :] * gain
                moved = (moved + rate * (beside - moved)) * sea[rows, :]
                if grown:
                    waves[step + 1, rows, lanes] = moved * growths[rows, lanes]
                else:
                    turned[rows, lanes] = moved
            if grown and chunk % 2:
                part = stokes_part(waves[step + 1, :, 128 * (chunk - 1) : 128 * (chunk + 1)], chunk // 2)
                drift = part if drift is None else drift + part
        return drift

    def push(flow, spin, drift, wet):
        return (keep * wet) * (flow + twist * spin * pltpu.roll(flow + drift, 32, 1))

    def find_growth(seen):
        seen = jnp.concatenate([seen, seen[:, 0:64]], axis=1)
        for chunk in range(SPEC // 256):
            lanes = slice(256 * chunk, 256 * (chunk + 1))
            growths[:, lanes] = 1.0 + jnp.dot(seen, swell_table[:, lanes], preferred_element_type=f32)

    def grow(seen, step):
        seen = jnp.concatenate([seen, seen[:, 0:64]], axis=1)
        for chunk in range(SPEC // 256):
            lanes = slice(256 * chunk, 256 * (chunk + 1))
            growth = jnp.dot(seen, swell_table[:, lanes], preferred_element_type=f32)
            values = turned[:, lanes] * (1.0 + growth)
            if step == STEPS:
                spectra_out[:, lanes] = values
            else:
                waves[step, :, lanes] = values
        if step == STEPS:
            return None
        send_halos(step, 0)
        return find_drift(step)

    def find_drift(step):
        drift = None
        for chunk in range(SPEC // 256):
            part = stokes_part(waves[step, :, 256 * chunk : 256 * (chunk + 1)], chunk)
            drift = part if drift is None else drift + part
        return sorted_drift(step, drift)

    def first_seen(message):
        high = round_half(message)
        pieces = jnp.where(low_half, pltpu.roll(high, 64, 1), message - high).astype(bf16)
        seen = jnp.dot(place_back, pieces, preferred_element_type=f32)
        flow_at_waves[0] = seen + pltpu.roll(seen, 64, 1)
        return seen.astype(bf16)

    def next_seen(step, message):
        high = round_half(message)
        pieces = jnp.where(low_half, high, message - high).astype(bf16)
        both = jnp.dot(place_back, pieces, preferred_element_type=f32)
        both = both + pltpu.roll(both, 64, 1)
        other = pltpu.roll(both, 32, 1)
        spin = jnp.where(zonal, both, other)
        wet = jnp.where(zonal, other, both)
        flow = push(flow_at_waves[step - 1], spin, drifts[step - 1], wet)
        flow_at_waves[step] = flow
        high = round_half(flow)
        return jnp.where(low_half, high, flow - high).astype(bf16)

    def spin_message(step):
        return jnp.where(zonal, spins[step], sea[...])

    loads[4].wait()
    start_flow = currents_ref[...].reshape(CELLS, 2 * NDEPTH)
    flows[0] = jnp.concatenate([start_flow, start_flow], axis=1)
    for load in loads[5:]:
        load.wait()
    drift = find_drift(0)

    greeted = sections - 1 + has_south.astype(jnp.int32) + has_north.astype(jnp.int32)
    pl.semaphore_wait(barrier, greeted)

    send_halos(0, 1)
    send_first(jnp.where(low_half, drift, flows[0]))
    send_halos(0, 0)

    receive_halos(0, 1)
    find_spin(0)
    send_pairs(1, spin_message(0))
    receive_halos(0, 0)
    advect(0)
    message = receive_first()
    flows[1] = push(flows[0], spins[0], jnp.where(low_half, message, pltpu.roll(message, 64, 1)), sea[...])
    send_halos(1, 1)
    send_pairs(2, grow(first_seen(message), 1))

    find_growth(next_seen(1, receive_pairs(1)))
    receive_halos(1, 1)
    find_spin(1)
    send_pairs(3, spin_message(1))
    receive_halos(1, 0)
    drift = advect(1, grown=True)
    send_halos(2, 0)
    send_pairs(4, sorted_drift(2, drift))
    flows[2] = push(flows[1], spins[1], receive_pairs(2), sea[...])
    send_halos(2, 1)

    for step in range(STEPS):
        sent_halos(step, 0)
        sent_halos(step, 1)
    for index in range(2 * STEPS - 1):
        sent_pairs(index)
    receive_halos(2, 0)
    advect(2)
    grow(next_seen(2, receive_pairs(3)), 3)
    receive_halos(2, 1)
    find_spin(2)
    currents_out[...] = push(flows[2], spins[2], receive_pairs(4), sea[...])[:, 0 : 2 * NDEPTH]


def store(waves_ref, flows_ref, waves_out, flows_out, sems):
    copies = [
        pltpu.make_async_copy(waves_ref, waves_out, sems.at[0]),
        pltpu.make_async_copy(flows_ref, flows_out, sems.at[1]),
    ]
    for copy in copies:
        copy.start()
    for copy in copies:
        copy.wait()


def solution(mesh):
    sections, bands = mesh.shape["sec"], mesh.shape["lat"]
    rates, stokes_table, swell_table = build_tables()
    share = CELLS // sections

    def per_device(spectra, turning, currents, drag_rates, land_mask, ocean_target):
        f32, bf16 = jnp.float32, jnp.bfloat16
        vmem = pl.BlockSpec(memory_space=pltpu.VMEM)
        hbm = pl.BlockSpec(memory_space=pltpu.HBM)
        operands = (
            spectra.reshape(CELLS, SPEC),
            turning,
            currents,
            drag_rates.reshape(1, NDEPTH),
            land_mask,
            ocean_target,
            jnp.asarray(rates),
            jnp.asarray(stokes_table),
            jnp.asarray(swell_table),
        )
        waves, flows = pl.pallas_call(
            lambda *refs: kernel(sections, bands, *refs),
            out_shape=(
                jax.ShapeDtypeStruct((CELLS, SPEC), f32),
                jax.ShapeDtypeStruct((CELLS, 2 * NDEPTH), f32),
            ),
            in_specs=[hbm] * 9,
            out_specs=(vmem, vmem),
            scratch_shapes=[
                pltpu.VMEM((STEPS, CELLS, SPEC), f32),
                pltpu.VMEM((STEPS, CELLS, 128), f32),
                pltpu.VMEM((STEPS, COLS, SPEC // 2), f32),
                pltpu.VMEM((STEPS, COLS, SPEC // 2), f32),
                pltpu.VMEM((STEPS, ROWS, SPEC // 2), f32),
                pltpu.VMEM((STEPS, ROWS, SPEC // 2), f32),
                pltpu.VMEM((STEPS, COLS, 128), f32),
                pltpu.VMEM((STEPS, COLS, 128), f32),
                pltpu.VMEM((STEPS, ROWS, 128), f32),
                pltpu.VMEM((STEPS, ROWS, 128), f32),
                pltpu.VMEM((STEPS, 2, ROWS, SPEC // 2), f32),
                pltpu.VMEM((STEPS, 2, ROWS, 128), f32),
                pltpu.VMEM((sections, share, 128), f32),
                pltpu.VMEM((sections, share, 128), f32),
                pltpu.VMEM((2 * STEPS - 2, sections, share // 2, 128), f32),
                pltpu.VMEM((2 * STEPS - 2, sections, share // 2, 128), f32),
                pltpu.VMEM((2 * STEPS - 2, CELLS, 128), f32),
                pltpu.VMEM((2, ROWS, SPEC), f32),
                pltpu.VMEM((STEPS, 2, COLS, SPEC // 2), f32),
                pltpu.VMEM((CELLS, SPEC), f32),
                pltpu.VMEM((CELLS, SPEC), f32),
                pltpu.VMEM((STEPS, CELLS, 128), f32),
                pltpu.VMEM((STEPS, CELLS, 128), f32),
                pltpu.VMEM((STEPS, CELLS, 128), f32),
                pltpu.VMEM((ROWS, COLS), f32),
                pltpu.VMEM((ROWS, COLS, 2 * NDEPTH), f32),
                pltpu.VMEM((1, NDEPTH), f32),
                pltpu.VMEM((ROWS, COLS), jnp.int32),
                pltpu.VMEM((ROWS, COLS), jnp.int32),
                pltpu.VMEM((8, SPEC), f32),
                pltpu.VMEM((SPEC, 128), bf16),
                pltpu.VMEM((6 * NDEPTH, SPEC), bf16),
                pltpu.VMEM((4, 8, 128), f32),
                pltpu.VMEM((CELLS, 128), f32),
                pltpu.VMEM((CELLS, 128), f32),
                pltpu.VMEM((CELLS, 128), f32),
                pltpu.SemaphoreType.DMA((9,)),
                pltpu.SemaphoreType.DMA((2 * STEPS, 4)),
                pltpu.SemaphoreType.DMA((2 * STEPS, 4)),
                pltpu.SemaphoreType.DMA((2 * STEPS - 1, sections)),
                pltpu.SemaphoreType.DMA((2 * STEPS - 1, sections)),
            ],
            compiler_params=pltpu.CompilerParams(
                collective_id=0, has_side_effects=True, vmem_limit_bytes=24 << 20
            ),
        )(*[pltpu.with_memory_space_constraint(x, pltpu.HBM) for x in operands])
        waves, flows = pl.pallas_call(
            store,
            out_shape=(
                jax.ShapeDtypeStruct((CELLS, SPEC), f32),
                jax.ShapeDtypeStruct((CELLS, 2 * NDEPTH), f32),
            ),
            in_specs=[vmem, vmem],
            out_specs=(hbm, hbm),
            scratch_shapes=[pltpu.SemaphoreType.DMA((2,))],
        )(*[pltpu.with_memory_space_constraint(x, pltpu.VMEM) for x in (waves, flows)])
        return waves.reshape(ROWS, COLS, SPEC), flows.reshape(ROWS, COLS, 2 * NDEPTH)

    return jax.shard_map(
        per_device,
        mesh=mesh,
        in_specs=(
            P("lat", "sec", None),
            P("lat", "sec"),
            P("lat", "sec", None),
            P(),
            P("lat", "sec"),
            P("lat", "sec"),
        ),
        out_specs=(P("lat", "sec", None), P("lat", "sec", None)),
        check_vma=False,
    )
```

```python
import math

import jax
import jax.numpy as jnp
import ml_dtypes
import numpy as np
from jax import lax
from jax.experimental import pallas as pl
from jax.experimental.pallas import tpu as pltpu
from jax.sharding import PartitionSpec as P

NFREQ = 24
NDIR = 32
NDEPTH = 32
STEPS = 3
ROWS = 4
COLS = 24
CELLS = ROWS * COLS
SPEC = NFREQ * NDIR
RING = 3

STOKES_SCALE = 0.1
OCEAN_DT = 0.3
CURRENT_GAIN = 0.2

MESH = pl.DeviceIdType.MESH


def halves(table):
    high = table.astype(ml_dtypes.bfloat16)
    low = (table - high.astype(np.float32)).astype(ml_dtypes.bfloat16)
    return high, low


def build_tables():
    f32 = np.float32
    fraction = np.arange(NFREQ, dtype=f32) / f32(NFREQ - 1)
    angles = (np.arange(NDIR, dtype=f32) + f32(0.5)) * f32(2.0 * math.pi / NDIR)
    east = np.cos(angles).astype(f32)
    north = np.sin(angles).astype(f32)
    compass = np.stack([east, north])
    courant = f32(0.1) + f32(0.3) * fraction
    depth_level = f32(0.5) + f32(NDEPTH - 2) * (f32(1.0) - fraction)
    levels = np.arange(NDEPTH, dtype=f32)
    weights = np.maximum(f32(1.0) - np.abs(levels[None, :] - depth_level[:, None]), f32(0.0))
    mean_weights = weights / np.sum(weights, axis=1, keepdims=True)
    x_rate = (courant[:, None] * east[None, :]).reshape(-1)
    y_rate = (courant[:, None] * north[None, :]).reshape(-1)
    turn_gain = f32(1.0) - f32(0.5) * fraction
    growth = f32(CURRENT_GAIN) * (f32(1.0) + fraction)
    stokes = (
        f32(STOKES_SCALE) * weights[:, None, None, :] * compass.T[None, :, :, None]
    ).reshape(SPEC, 2 * NDEPTH)
    swell = (
        growth[None, None, :, None] * mean_weights.T[None, :, :, None] * compass[:, None, None, :]
    ).reshape(2 * NDEPTH, SPEC)
    rates = np.zeros((8, SPEC), f32)
    rates[0] = f32(1.0) - np.abs(x_rate) - np.abs(y_rate)
    rates[1] = np.abs(x_rate)
    rates[2] = np.abs(y_rate)
    rates[3] = np.repeat(turn_gain, NDIR)
    stokes_table = np.concatenate(halves(stokes), axis=1)
    swell_high, swell_low = halves(swell)
    swell_table = np.concatenate([swell_high, swell_high, swell_low], axis=0)
    return rates, stokes_table, swell_table


def iota(shape, dim):
    return lax.broadcasted_iota(jnp.int32, shape, dim)


def round_half(x):
    return x.astype(jnp.bfloat16).astype(jnp.float32)


def kernel(
    sections,
    bands,
    spectra_hbm,
    turning_hbm,
    currents_hbm,
    drag_hbm,
    land_hbm,
    target_hbm,
    rates_hbm,
    stokes_hbm,
    swell_hbm,
    spectra_out,
    currents_out,
    waves,
    flows,
    wave_south,
    wave_north,
    wave_west,
    wave_east,
    flow_south,
    flow_north,
    flow_west,
    flow_east,
    wave_edges,
    flow_edges,
    outgoing,
    arrived,
    half_out,
    half_in,
    unpacked,
    edge_lines,
    band_edges,
    turned,
    growths,
    spins,
    drifts,
    flow_at_waves,
    turning_ref,
    currents_ref,
    drag_ref,
    land_ref,
    target_ref,
    rates_ref,
    stokes_table,
    swell_table,
    tiny,
    turn_size,
    turn_sign,
    sea,
    load_sem,
    halo_send,
    halo_recv,
    pair_send,
    pair_recv,
):
    f32, bf16 = jnp.float32, jnp.bfloat16
    share = CELLS // sections
    sec = lax.axis_index("sec")
    lat = lax.axis_index("lat")
    has_west, has_east = sec > 0, sec < sections - 1
    has_south, has_north = lat > 0, lat < bands - 1

    lines = sections // RING
    line, spot = lax.div(sec, RING), lax.rem(sec, RING)
    hops = sorted(
        ((over, along) for over in range(lines) for along in range(RING) if over or along),
        key=lambda hop: (hop[1] == 0, -min(hop[0], lines - hop[0])),
    )

    def peer_of(hop):
        return RING * lax.rem(line + hop[0], lines) + lax.rem(spot + hop[1], RING)

    barrier = pltpu.get_barrier_semaphore()
    for hop in hops:
        peer = peer_of(hop)
        pl.semaphore_signal(barrier, inc=1, device_id={"sec": peer}, device_id_type=MESH)

    @pl.when(has_south)
    def _():
        pl.semaphore_signal(barrier, inc=1, device_id={"lat": lat - 1}, device_id_type=MESH)

    @pl.when(has_north)
    def _():
        pl.semaphore_signal(barrier, inc=1, device_id={"lat": lat + 1}, device_id_type=MESH)

    pairs = (
        (turning_hbm, turning_ref),
        (drag_hbm, drag_ref),
        (land_hbm, land_ref),
        (target_hbm, target_ref),
        (currents_hbm, currents_ref),
        (rates_hbm, rates_ref),
        (spectra_hbm, waves.at[0]),
        (stokes_hbm, stokes_table),
        (swell_hbm, swell_table),
    )
    loads = [pltpu.make_async_copy(there, here, load_sem.at[i]) for i, (there, here) in enumerate(pairs)]
    for load in loads:
        load.start()

    for there, halos in (
        (has_south, (wave_south, flow_south)),
        (has_north, (wave_north, flow_north)),
        (has_west, (wave_west, flow_west)),
        (has_east, (wave_east, flow_east)),
    ):

        @pl.when(jnp.logical_not(there))
        def _():
            for halo in halos:
                halo[...] = jnp.zeros_like(halo)

    tiny[...] = jnp.zeros_like(tiny)
    for load in loads[:4]:
        load.wait()
    tiny[0, 0:ROWS, 0:COLS] = turning_ref[...]
    tiny[1, 0:ROWS, 0:COLS] = land_ref[...].astype(f32)
    tiny[2, 0:ROWS, 0:COLS] = target_ref[...].astype(f32)
    tiny[3, 0:1, 0:NDEPTH] = 1.0 - drag_ref[...]

    lane_row = iota((1, 128), 1)
    target_rows = tiny[2]
    targets = jnp.full((1, 128), 99.0, f32)
    for y in range(ROWS):
        row = target_rows[y : y + 1, :]
        moved = pltpu.roll(row, COLS * y, 1) if y else row
        inside = jnp.logical_and(lane_row >= COLS * y, lane_row < COLS * (y + 1))
        targets = jnp.where(inside, moved, targets)
    matches = (iota((16, 128), 0).astype(f32) == targets).astype(f32)
    earlier = (iota((128, 128), 0) < iota((128, 128), 1)).astype(f32)
    before = jnp.dot(matches.astype(bf16), earlier.astype(bf16), preferred_element_type=f32)
    rank = jnp.sum(matches * before, axis=0, keepdims=True)
    place_of = targets * share + rank
    place = (iota((128, 128), 0).astype(f32) == place_of).astype(f32)
    place_back = jnp.transpose(place)[0:CELLS, 0:CELLS].astype(bf16)
    place = place[0:CELLS, 0:CELLS].astype(bf16)

    turn_columns = jnp.transpose(tiny[0])
    sea_columns = jnp.transpose(tiny[1])
    for y in range(ROWS):
        rows = slice(COLS * y, COLS * (y + 1))
        turn = jnp.broadcast_to(turn_columns[0:COLS, y : y + 1], (COLS, 128))
        turn_size[rows, :] = jnp.abs(turn)
        turn_sign[rows, :] = turn
        sea[rows, :] = jnp.broadcast_to(sea_columns[0:COLS, y : y + 1], (COLS, 128))

    keep = tiny[3, 0:1, :]
    keep = keep + pltpu.roll(keep, 32, 1)
    keep = keep + pltpu.roll(keep, 64, 1)

    lane = iota((COLS, 128), 1)
    column = iota((COLS, 128), 0)
    first_column = column == 0
    last_column = column == COLS - 1
    direction = lane & (NDIR - 1)
    goes_east = jnp.logical_or(direction < NDIR // 4, direction >= 3 * NDIR // 4)
    goes_north = direction < NDIR // 2
    first_direction = direction == 0
    last_direction = direction == NDIR - 1
    full_lane = iota((CELLS, 128), 1)
    low_half = full_lane < 64
    zonal = (full_lane & 63) < 32
    low_rows = iota((share // 2, 128), 1) < 64
    zonal_row = (lane & 63) < 32
    twist = jnp.where(zonal, OCEAN_DT, -OCEAN_DT)
    global_row = (lat * ROWS).astype(f32)

    def halo_copies(step, is_flow):
        edges = (flow_edges if is_flow else wave_edges).at[step]
        if is_flow:
            first = flows.at[step, pl.ds(0, COLS)]
            final = flows.at[step, pl.ds(CELLS - COLS, COLS)]
        else:
            first, final = band_edges.at[step, 0], band_edges.at[step, 1]
        south, north, west, east = (
            (flow_south, flow_north, flow_west, flow_east)
            if is_flow
            else (wave_south, wave_north, wave_west, wave_east)
        )
        index = 2 * step + is_flow
        plan = (
            (has_west, has_east, edges.at[0], east, {"sec": sec - 1}),
            (has_east, has_west, edges.at[1], west, {"sec": sec + 1}),
            (has_south, has_north, first, north, {"lat": lat - 1}),
            (has_north, has_south, final, south, {"lat": lat + 1}),
        )
        for k, (sends, receives, source, halo, device) in enumerate(plan):
            copy = lambda source=source, halo=halo, device=device, k=k: pltpu.make_async_remote_copy(
                src_ref=source,
                dst_ref=halo.at[step],
                send_sem=halo_send.at[index, k],
                recv_sem=halo_recv.at[index, k],
                device_id=device,
                device_id_type=MESH,
            )
            yield sends, receives, copy

    def pack(tiles, needed):
        return [
            jnp.where(needed[0 : tiles[0].shape[0]], tiles[2 * c], pltpu.roll(tiles[2 * c + 1], 16, 1))
            for c in range(SPEC // 256)
        ]

    def unpack(halo, chunk):
        return pltpu.roll(halo, 112, 1) if chunk % 2 else halo

    def half_lanes(chunk):
        return slice(128 * (chunk // 2), 128 * (chunk // 2 + 1))

    def tiles_of(values):
        return [values[:, 128 * c : 128 * (c + 1)] for c in range(SPEC // 128)]

    def ready_halos(step, is_flow):
        if is_flow:
            for y in range(ROWS):
                flow_edges[step, 0, y : y + 1, :] = flows[step, COLS * y : COLS * y + 1, :]
                flow_edges[step, 1, y : y + 1, :] = flows[step, COLS * (y + 1) - 1 : COLS * (y + 1), :]
        else:
            for y in range(ROWS):
                edge_lines[0, y : y + 1, :] = waves[step, COLS * y : COLS * y + 1, :]
                edge_lines[1, y : y + 1, :] = waves[step, COLS * (y + 1) - 1 : COLS * (y + 1), :]
            places = (
                (wave_edges, 0, edge_lines[0], jnp.logical_not(goes_east)),
                (wave_edges, 1, edge_lines[1], goes_east),
                (band_edges, 0, waves[step, 0:COLS, :], jnp.logical_not(goes_north)),
                (band_edges, 1, waves[step, CELLS - COLS : CELLS, :], goes_north),
            )
            for edges, side, values, needed in places:
                for c, tile in enumerate(pack(tiles_of(values), needed)):
                    edges[step, side, :, 128 * c : 128 * (c + 1)] = tile

    def send_halos(step, is_flow, ready=False):
        if not ready:
            ready_halos(step, is_flow)
        for sends, _, copy in halo_copies(step, is_flow):

            @pl.when(sends)
            def _():
                copy().start()

    def receive_halos(step, is_flow):
        for _, receives, copy in halo_copies(step, is_flow):

            @pl.when(receives)
            def _():
                copy().wait_recv()

    def pair_copy(index, k):
        peer = peer_of(hops[k])
        return pltpu.make_async_remote_copy(
            src_ref=half_out.at[index - 1, peer] if index else outgoing.at[peer],
            dst_ref=half_in.at[index - 1, sec] if index else arrived.at[sec],
            send_sem=pair_send.at[index],
            recv_sem=pair_recv.at[index],
            device_id={"sec": peer},
            device_id_type=MESH,
        )

    def start_pairs(index):
        for k in range(sections - 1):
            pair_copy(index, k).start()

    def ready_first(message):
        outgoing[...] = message.reshape(sections, share, 128)
        arrived[sec] = outgoing[sec]

    def all_pairs(index):
        others = pl.ds(0, sections - 1)
        return pltpu.make_async_remote_copy(
            src_ref=half_out.at[index - 1, others] if index else outgoing.at[others],
            dst_ref=half_in.at[index - 1, others] if index else arrived.at[others],
            send_sem=pair_send.at[index],
            recv_sem=pair_recv.at[index],
            device_id={"sec": peer_of(hops[0])},
            device_id_type=MESH,
        )

    def receive(index):
        all_pairs(index).wait_recv()

    def receive_first():
        receive(0)
        return arrived[...].reshape(CELLS, 128)

    def send_pairs(index, message):
        folded = jnp.where(low_half, message, pltpu.roll(message, CELLS - share // 2, 0))
        for k in range(sections):
            half_out[index - 1, k] = folded[share * k : share * k + share // 2, :]
        start_pairs(index)
        half_in[index - 1, sec] = half_out[index - 1, sec]

    def receive_pairs(index):
        receive(index)
        for k in range(sections):
            rows = half_in[index - 1, k]
            other = pltpu.roll(rows, 64, 1)
            unpacked[index - 1, share * k : share * k + share // 2, :] = jnp.where(low_rows, rows, other)
            unpacked[index - 1, share * k + share // 2 : share * (k + 1), :] = jnp.where(low_rows, other, rows)
        return unpacked[index - 1]

    def sent_halos(step, is_flow):
        for sends, _, copy in halo_copies(step, is_flow):

            @pl.when(sends)
            def _():
                copy().wait_send()

    def sent_pairs(index):
        all_pairs(index).wait_send()

    def stokes_part(values, chunk):
        high = values.astype(bf16)
        low = (values - high.astype(f32)).astype(bf16)
        both = jnp.concatenate([high, low], axis=0)
        return jnp.dot(both, stokes_table[256 * chunk : 256 * (chunk + 1), :], preferred_element_type=f32)

    def sorted_drift(step, drift):
        drift = drift[0:CELLS] + drift[CELLS:]
        drift = drift + pltpu.roll(drift, 64, 1)
        drifts[step] = drift
        high = round_half(drift)
        pieces = jnp.where(low_half, high, drift - high).astype(bf16)
        drift = jnp.dot(place, pieces, preferred_element_type=f32)
        return drift + pltpu.roll(drift, 64, 1)

    def neighbours(own, halos, step, y, lanes, chunk=None):
        south, north, west, east = halos
        rows = slice(COLS * y, COLS * (y + 1))
        here = own[step, rows, lanes]
        edge = lanes if chunk is None else half_lanes(chunk)
        fit = (lambda halo: halo) if chunk is None else (lambda halo: unpack(halo, chunk))
        return (
            here,
            jnp.where(first_column, fit(west[step, y : y + 1, edge]), pltpu.roll(here, 1, 0)),
            jnp.where(last_column, fit(east[step, y : y + 1, edge]), pltpu.roll(here, COLS - 1, 0)),
            own[step, COLS * (y - 1) : COLS * y, lanes] if y else fit(south[step, :, edge]),
            own[step, COLS * (y + 1) : COLS * (y + 2), lanes] if y < ROWS - 1 else fit(north[step, :, edge]),
        )

    def find_spin(step):
        for y in range(ROWS):
            _, west, east, south, north = neighbours(
                flows, (flow_south, flow_north, flow_west, flow_east), step, y, slice(0, 128)
            )
            sheared = jnp.where(zonal_row, south - north, east - west)
            spin = 0.5 * (sheared + pltpu.roll(sheared, 32, 1))
            spins[step, COLS * y : COLS * (y + 1), :] = spin + (0.2 + 0.6 * (global_row + y) / (ROWS * bands))

    def advect(step, grown=False):
        drift = None
        for chunk in range(SPEC // 128):
            lanes = slice(128 * chunk, 128 * (chunk + 1))
            stay = rates_ref[0:1, lanes]
            rate_x = rates_ref[1:2, lanes]
            rate_y = rates_ref[2:3, lanes]
            gain = rates_ref[3:4, lanes]
            for y in range(ROWS):
                rows = slice(COLS * y, COLS * (y + 1))
                here, west, east, south, north = neighbours(
                    waves, (wave_south, wave_north, wave_west, wave_east), step, y, lanes, chunk
                )
                moved = (
                    stay * here
                    + rate_x * jnp.where(goes_east, west, east)
                    + rate_y * jnp.where(goes_north, south, north)
                )
                behind = jnp.where(first_direction, pltpu.roll(moved, 97, 1), pltpu.roll(moved, 1, 1))
                forward = jnp.where(last_direction, pltpu.roll(moved, 31, 1), pltpu.roll(moved, 127, 1))
                beside = jnp.where(turn_sign[rows, :] > 0.0, behind, forward)
                rate = turn_size[rows, :] * gain
                moved = (moved + rate * (beside - moved)) * sea[rows, :]
                if grown:
                    waves[step + 1, rows, lanes] = moved * growths[rows, lanes]
                else:
                    turned[rows, lanes] = moved
            if grown and chunk % 2:
                part = stokes_part(waves[step + 1, :, 128 * (chunk - 1) : 128 * (chunk + 1)], chunk // 2)
                drift = part if drift is None else drift + part
        return drift

    def push(flow, spin, drift, wet):
        return (keep * wet) * (flow + twist * spin * pltpu.roll(flow + drift, 32, 1))

    def find_growth(seen):
        seen = jnp.concatenate([seen, seen[:, 0:64]], axis=1)
        for chunk in range(SPEC // 256):
            lanes = slice(256 * chunk, 256 * (chunk + 1))
            growths[:, lanes] = 1.0 + jnp.dot(seen, swell_table[:, lanes], preferred_element_type=f32)

    def grow(seen, step):
        seen = jnp.concatenate([seen, seen[:, 0:64]], axis=1)
        for chunk in range(SPEC // 256):
            lanes = slice(256 * chunk, 256 * (chunk + 1))
            growth = jnp.dot(seen, swell_table[:, lanes], preferred_element_type=f32)
            values = turned[:, lanes] * (1.0 + growth)
            if step == STEPS:
                spectra_out[:, lanes] = values
            else:
                waves[step, :, lanes] = values
        if step == STEPS:
            return None
        send_halos(step, 0)
        return find_drift(step)

    def find_drift(step):
        drift = None
        for chunk in range(SPEC // 256):
            part = stokes_part(waves[step, :, 256 * chunk : 256 * (chunk + 1)], chunk)
            drift = part if drift is None else drift + part
        return sorted_drift(step, drift)

    def first_seen(message):
        high = round_half(message)
        pieces = jnp.where(low_half, pltpu.roll(high, 64, 1), message - high).astype(bf16)
        seen = jnp.dot(place_back, pieces, preferred_element_type=f32)
        flow_at_waves[0] = seen + pltpu.roll(seen, 64, 1)
        return seen.astype(bf16)

    def next_seen(step, message):
        high = round_half(message)
        pieces = jnp.where(low_half, high, message - high).astype(bf16)
        both = jnp.dot(place_back, pieces, preferred_element_type=f32)
        both = both + pltpu.roll(both, 64, 1)
        other = pltpu.roll(both, 32, 1)
        spin = jnp.where(zonal, both, other)
        wet = jnp.where(zonal, other, both)
        flow = push(flow_at_waves[step - 1], spin, drifts[step - 1], wet)
        flow_at_waves[step] = flow
        high = round_half(flow)
        return jnp.where(low_half, high, flow - high).astype(bf16)

    def spin_message(step):
        return jnp.where(zonal, spins[step], sea[...])

    loads[4].wait()
    start_flow = currents_ref[...].reshape(CELLS, 2 * NDEPTH)
    flows[0] = jnp.concatenate([start_flow, start_flow], axis=1)
    for load in loads[5:]:
        load.wait()
    ready_halos(0, 1)
    ready_halos(0, 0)
    ready_first(jnp.where(low_half, find_drift(0), flows[0]))

    greeted = sections - 1 + has_south.astype(jnp.int32) + has_north.astype(jnp.int32)
    pl.semaphore_wait(barrier, greeted)

    start_pairs(0)
    send_halos(0, 1, ready=True)
    send_halos(0, 0, ready=True)

    receive_halos(0, 1)
    find_spin(0)
    send_pairs(1, spin_message(0))
    receive_halos(0, 0)
    advect(0)
    message = receive_first()
    flows[1] = push(flows[0], spins[0], jnp.where(low_half, message, pltpu.roll(message, 64, 1)), sea[...])
    send_halos(1, 1)
    send_pairs(2, grow(first_seen(message), 1))

    find_growth(next_seen(1, receive_pairs(1)))
    receive_halos(1, 1)
    find_spin(1)
    send_pairs(3, spin_message(1))
    receive_halos(1, 0)
    drift = advect(1, grown=True)
    send_halos(2, 0)
    send_pairs(4, sorted_drift(2, drift))
    flows[2] = push(flows[1], spins[1], receive_pairs(2), sea[...])
    send_halos(2, 1)

    for step in range(STEPS):
        sent_halos(step, 0)
        sent_halos(step, 1)
    for index in range(2 * STEPS - 1):
        sent_pairs(index)
    receive_halos(2, 0)
    advect(2)
    grow(next_seen(2, receive_pairs(3)), 3)
    receive_halos(2, 1)
    find_spin(2)
    currents_out[...] = push(flows[2], spins[2], receive_pairs(4), sea[...])[:, 0 : 2 * NDEPTH]


def store(waves_ref, flows_ref, waves_out, flows_out, sems):
    copies = [
        pltpu.make_async_copy(waves_ref, waves_out, sems.at[0]),
        pltpu.make_async_copy(flows_ref, flows_out, sems.at[1]),
    ]
    for copy in copies:
        copy.start()
    for copy in copies:
        copy.wait()


def solution(mesh):
    sections, bands = mesh.shape["sec"], mesh.shape["lat"]
    rates, stokes_table, swell_table = build_tables()
    share = CELLS // sections

    def per_device(spectra, turning, currents, drag_rates, land_mask, ocean_target):
        f32, bf16 = jnp.float32, jnp.bfloat16
        vmem = pl.BlockSpec(memory_space=pltpu.VMEM)
        hbm = pl.BlockSpec(memory_space=pltpu.HBM)
        operands = (
            spectra.reshape(CELLS, SPEC),
            turning,
            currents,
            drag_rates.reshape(1, NDEPTH),
            land_mask,
            ocean_target,
            jnp.asarray(rates),
            jnp.asarray(stokes_table),
            jnp.asarray(swell_table),
        )
        waves, flows = pl.pallas_call(
            lambda *refs: kernel(sections, bands, *refs),
            out_shape=(
                jax.ShapeDtypeStruct((CELLS, SPEC), f32),
                jax.ShapeDtypeStruct((CELLS, 2 * NDEPTH), f32),
            ),
            in_specs=[hbm] * 9,
            out_specs=(vmem, vmem),
            scratch_shapes=[
                pltpu.VMEM((STEPS, CELLS, SPEC), f32),
                pltpu.VMEM((STEPS, CELLS, 128), f32),
                pltpu.VMEM((STEPS, COLS, SPEC // 2), f32),
                pltpu.VMEM((STEPS, COLS, SPEC // 2), f32),
                pltpu.VMEM((STEPS, ROWS, SPEC // 2), f32),
                pltpu.VMEM((STEPS, ROWS, SPEC // 2), f32),
                pltpu.VMEM((STEPS, COLS, 128), f32),
                pltpu.VMEM((STEPS, COLS, 128), f32),
                pltpu.VMEM((STEPS, ROWS, 128), f32),
                pltpu.VMEM((STEPS, ROWS, 128), f32),
                pltpu.VMEM((STEPS, 2, ROWS, SPEC // 2), f32),
                pltpu.VMEM((STEPS, 2, ROWS, 128), f32),
                pltpu.VMEM((sections, share, 128), f32),
                pltpu.VMEM((sections, share, 128), f32),
                pltpu.VMEM((2 * STEPS - 2, sections, share // 2, 128), f32),
                pltpu.VMEM((2 * STEPS - 2, sections, share // 2, 128), f32),
                pltpu.VMEM((2 * STEPS - 2, CELLS, 128), f32),
                pltpu.VMEM((2, ROWS, SPEC), f32),
                pltpu.VMEM((STEPS, 2, COLS, SPEC // 2), f32),
                pltpu.VMEM((CELLS, SPEC), f32),
                pltpu.VMEM((CELLS, SPEC), f32),
                pltpu.VMEM((STEPS, CELLS, 128), f32),
                pltpu.VMEM((STEPS, CELLS, 128), f32),
                pltpu.VMEM((STEPS, CELLS, 128), f32),
                pltpu.VMEM((ROWS, COLS), f32),
                pltpu.VMEM((ROWS, COLS, 2 * NDEPTH), f32),
                pltpu.VMEM((1, NDEPTH), f32),
                pltpu.VMEM((ROWS, COLS), jnp.int32),
                pltpu.VMEM((ROWS, COLS), jnp.int32),
                pltpu.VMEM((8, SPEC), f32),
                pltpu.VMEM((SPEC, 128), bf16),
                pltpu.VMEM((6 * NDEPTH, SPEC), bf16),
                pltpu.VMEM((4, 8, 128), f32),
                pltpu.VMEM((CELLS, 128), f32),
                pltpu.VMEM((CELLS, 128), f32),
                pltpu.VMEM((CELLS, 128), f32),
                pltpu.SemaphoreType.DMA((9,)),
                pltpu.SemaphoreType.DMA((2 * STEPS, 4)),
                pltpu.SemaphoreType.DMA((2 * STEPS, 4)),
                pltpu.SemaphoreType.DMA((2 * STEPS - 1,)),
                pltpu.SemaphoreType.DMA((2 * STEPS - 1,)),
            ],
            compiler_params=pltpu.CompilerParams(
                collective_id=0, has_side_effects=True, vmem_limit_bytes=24 << 20
            ),
        )(*[pltpu.with_memory_space_constraint(x, pltpu.HBM) for x in operands])
        waves, flows = pl.pallas_call(
            store,
            out_shape=(
                jax.ShapeDtypeStruct((CELLS, SPEC), f32),
                jax.ShapeDtypeStruct((CELLS, 2 * NDEPTH), f32),
            ),
            in_specs=[vmem, vmem],
            out_specs=(hbm, hbm),
            scratch_shapes=[pltpu.SemaphoreType.DMA((2,))],
        )(*[pltpu.with_memory_space_constraint(x, pltpu.VMEM) for x in (waves, flows)])
        return waves.reshape(ROWS, COLS, SPEC), flows.reshape(ROWS, COLS, 2 * NDEPTH)

    return jax.shard_map(
        per_device,
        mesh=mesh,
        in_specs=(
            P("lat", "sec", None),
            P("lat", "sec"),
            P("lat", "sec", None),
            P(),
            P("lat", "sec"),
            P("lat", "sec"),
        ),
        out_specs=(P("lat", "sec", None), P("lat", "sec", None)),
        check_vma=False,
    )
```

```python
import math

import jax
import jax.numpy as jnp
import ml_dtypes
import numpy as np
from jax import lax
from jax.experimental import pallas as pl
from jax.experimental.pallas import tpu as pltpu
from jax.sharding import PartitionSpec as P

NFREQ = 24
NDIR = 32
NDEPTH = 32
STEPS = 3
ROWS = 4
COLS = 24
CELLS = ROWS * COLS
SPEC = NFREQ * NDIR
RING = 3

STOKES_SCALE = 0.1
OCEAN_DT = 0.3
CURRENT_GAIN = 0.2

MESH = pl.DeviceIdType.MESH


def halves(table):
    high = table.astype(ml_dtypes.bfloat16)
    low = (table - high.astype(np.float32)).astype(ml_dtypes.bfloat16)
    return high, low


def build_tables():
    f32 = np.float32
    fraction = np.arange(NFREQ, dtype=f32) / f32(NFREQ - 1)
    angles = (np.arange(NDIR, dtype=f32) + f32(0.5)) * f32(2.0 * math.pi / NDIR)
    east = np.cos(angles).astype(f32)
    north = np.sin(angles).astype(f32)
    compass = np.stack([east, north])
    courant = f32(0.1) + f32(0.3) * fraction
    depth_level = f32(0.5) + f32(NDEPTH - 2) * (f32(1.0) - fraction)
    levels = np.arange(NDEPTH, dtype=f32)
    weights = np.maximum(f32(1.0) - np.abs(levels[None, :] - depth_level[:, None]), f32(0.0))
    mean_weights = weights / np.sum(weights, axis=1, keepdims=True)
    x_rate = (courant[:, None] * east[None, :]).reshape(-1)
    y_rate = (courant[:, None] * north[None, :]).reshape(-1)
    turn_gain = f32(1.0) - f32(0.5) * fraction
    growth = f32(CURRENT_GAIN) * (f32(1.0) + fraction)
    stokes = (
        f32(STOKES_SCALE) * weights[:, None, None, :] * compass.T[None, :, :, None]
    ).reshape(SPEC, 2 * NDEPTH)
    swell = (
        growth[None, None, :, None] * mean_weights.T[None, :, :, None] * compass[:, None, None, :]
    ).reshape(2 * NDEPTH, SPEC)
    rates = np.zeros((8, SPEC), f32)
    rates[0] = f32(1.0) - np.abs(x_rate) - np.abs(y_rate)
    rates[1] = np.abs(x_rate)
    rates[2] = np.abs(y_rate)
    rates[3] = np.repeat(turn_gain, NDIR)
    stokes_table = np.concatenate(halves(stokes), axis=1)
    swell_high, swell_low = halves(swell)
    swell_table = np.concatenate([swell_high, swell_high, swell_low], axis=0)
    return rates, stokes_table, swell_table


def iota(shape, dim):
    return lax.broadcasted_iota(jnp.int32, shape, dim)


def round_half(x):
    return x.astype(jnp.bfloat16).astype(jnp.float32)


def kernel(
    sections,
    bands,
    spectra_hbm,
    turning_hbm,
    currents_hbm,
    drag_hbm,
    land_hbm,
    target_hbm,
    rates_hbm,
    stokes_hbm,
    swell_hbm,
    spectra_out,
    currents_out,
    waves,
    flows,
    wave_bands,
    wave_sides,
    flow_bands,
    flow_sides,
    wave_edges,
    flow_edges,
    outgoing,
    arrived,
    half_out,
    half_in,
    unpacked,
    edge_lines,
    band_edges,
    zeros,
    no_side,
    turned,
    growths,
    spins,
    drifts,
    flow_at_waves,
    turning_ref,
    currents_ref,
    drag_ref,
    land_ref,
    target_ref,
    rates_ref,
    stokes_table,
    swell_table,
    tiny,
    turn_size,
    turn_sign,
    sea,
    load_sem,
    halo_send,
    halo_recv,
    pair_send,
    pair_recv,
):
    f32, bf16 = jnp.float32, jnp.bfloat16
    share = CELLS // sections
    sec = lax.axis_index("sec")
    lat = lax.axis_index("lat")
    has_west, has_east = sec > 0, sec < sections - 1
    has_south, has_north = lat > 0, lat < bands - 1

    lines = sections // RING
    line, spot = lax.div(sec, RING), lax.rem(sec, RING)
    hops = sorted(
        ((over, along) for over in range(lines) for along in range(RING) if over or along),
        key=lambda hop: (hop[1] == 0, -min(hop[0], lines - hop[0])),
    )

    def peer_of(hop):
        far, near = line + hop[0], spot + hop[1]
        far = jnp.where(far >= lines, far - lines, far)
        return RING * far + jnp.where(near >= RING, near - RING, near)

    peers = [peer_of(hop) for hop in hops]

    barrier = pltpu.get_barrier_semaphore()
    for peer in peers:
        pl.semaphore_signal(barrier, inc=1, device_id={"sec": peer}, device_id_type=MESH)

    for there, other in ((has_south, lat - 1), (has_north, lat + 1)):

        @pl.when(there)
        def _():
            pl.semaphore_signal(barrier, inc=1, device_id={"lat": other}, device_id_type=MESH)

    pairs = (
        (turning_hbm, turning_ref),
        (drag_hbm, drag_ref),
        (land_hbm, land_ref),
        (target_hbm, target_ref),
        (currents_hbm, currents_ref),
        (rates_hbm, rates_ref),
        (spectra_hbm, waves.at[0]),
        (stokes_hbm, stokes_table),
        (swell_hbm, swell_table),
    )
    loads = [pltpu.make_async_copy(there, here, load_sem.at[i]) for i, (there, here) in enumerate(pairs)]
    for load in loads:
        load.start()

    zeros[...] = jnp.zeros_like(zeros)
    no_side[...] = jnp.zeros_like(no_side)
    for step in range(STEPS):
        for kind, (bands_in, sides_in) in enumerate(((wave_bands, wave_sides), (flow_bands, flow_sides))):
            width = bands_in.shape[-1]
            for there, halo, k in (
                (has_west, sides_in.at[step, 0], 0),
                (has_east, sides_in.at[step, 1], 0),
                (has_south, bands_in.at[step, 0], 1),
                (has_north, bands_in.at[step, 1], 1),
            ):

                @pl.when(jnp.logical_not(there))
                def _():
                    empty = zeros.at[pl.ds(0, COLS), pl.ds(0, width)] if k else no_side.at[:, pl.ds(0, width)]
                    pltpu.make_async_copy(empty, halo, halo_recv.at[2 * step + kind, k]).start()

    tiny[...] = jnp.zeros_like(tiny)
    for load in loads[:4]:
        load.wait()
    tiny[0, 0:ROWS, 0:COLS] = turning_ref[...]
    tiny[1, 0:ROWS, 0:COLS] = land_ref[...].astype(f32)
    tiny[2, 0:ROWS, 0:COLS] = target_ref[...].astype(f32)
    tiny[3, 0:1, 0:NDEPTH] = 1.0 - drag_ref[...]

    lane_row = iota((1, 128), 1)
    target_rows = tiny[2]
    targets = jnp.full((1, 128), 99.0, f32)
    for y in range(ROWS):
        row = target_rows[y : y + 1, :]
        moved = pltpu.roll(row, COLS * y, 1) if y else row
        inside = jnp.logical_and(lane_row >= COLS * y, lane_row < COLS * (y + 1))
        targets = jnp.where(inside, moved, targets)
    matches = (iota((16, 128), 0).astype(f32) == targets).astype(f32)
    earlier = (iota((128, 128), 0) < iota((128, 128), 1)).astype(f32)
    before = jnp.dot(matches.astype(bf16), earlier.astype(bf16), preferred_element_type=f32)
    rank = jnp.sum(matches * before, axis=0, keepdims=True)
    place_of = targets * share + rank
    place = (iota((128, 128), 0).astype(f32) == place_of).astype(f32)
    place_back = jnp.transpose(place)[0:CELLS, 0:CELLS].astype(bf16)
    place = place[0:CELLS, 0:CELLS].astype(bf16)

    turn_columns = jnp.transpose(tiny[0])
    sea_columns = jnp.transpose(tiny[1])
    for y in range(ROWS):
        rows = slice(COLS * y, COLS * (y + 1))
        turn = jnp.broadcast_to(turn_columns[0:COLS, y : y + 1], (COLS, 128))
        turn_size[rows, :] = jnp.abs(turn)
        turn_sign[rows, :] = turn
        sea[rows, :] = jnp.broadcast_to(sea_columns[0:COLS, y : y + 1], (COLS, 128))

    keep = tiny[3, 0:1, :]
    keep = keep + pltpu.roll(keep, 32, 1)
    keep = keep + pltpu.roll(keep, 64, 1)

    lane = iota((COLS, 128), 1)
    column = iota((COLS, 128), 0)
    first_column = column == 0
    last_column = column == COLS - 1
    direction = lane & (NDIR - 1)
    goes_east = jnp.logical_or(direction < NDIR // 4, direction >= 3 * NDIR // 4)
    goes_north = direction < NDIR // 2
    first_direction = direction == 0
    last_direction = direction == NDIR - 1
    full_lane = iota((CELLS, 128), 1)
    low_half = full_lane < 64
    zonal = (full_lane & 63) < 32
    low_rows = iota((share // 2, 128), 1) < 64
    zonal_row = (lane & 63) < 32
    twist = jnp.where(zonal, OCEAN_DT, -OCEAN_DT)
    global_row = (lat * ROWS).astype(f32)

    def halo_copies(step, is_flow):
        bands_in, sides_in = (flow_bands, flow_sides) if is_flow else (wave_bands, wave_sides)
        edges = (flow_edges if is_flow else wave_edges).at[step]
        if is_flow:
            first = flows.at[step, pl.ds(0, COLS)]
            final = flows.at[step, pl.ds(CELLS - COLS, COLS)]
        else:
            first, final = band_edges.at[step, 0], band_edges.at[step, 1]
        index = 2 * step + is_flow
        plan = (
            (has_west, edges.at[0], sides_in.at[step, 1], 0, {"sec": sec - 1}),
            (has_east, edges.at[1], sides_in.at[step, 0], 0, {"sec": sec + 1}),
            (has_south, first, bands_in.at[step, 1], 1, {"lat": lat - 1}),
            (has_north, final, bands_in.at[step, 0], 1, {"lat": lat + 1}),
        )
        for number, (there, source, halo, k, device) in enumerate(plan):
            yield there, lambda: pltpu.make_async_remote_copy(
                src_ref=source,
                dst_ref=halo,
                send_sem=halo_send.at[index, number],
                recv_sem=halo_recv.at[index, k],
                device_id=device,
                device_id_type=MESH,
            )

    def pack(tiles, needed):
        return [
            jnp.where(needed[0 : tiles[0].shape[0]], tiles[2 * c], pltpu.roll(tiles[2 * c + 1], 16, 1))
            for c in range(SPEC // 256)
        ]

    def unpack(halo, chunk):
        return pltpu.roll(halo, 112, 1) if chunk % 2 else halo

    def half_lanes(chunk):
        return slice(128 * (chunk // 2), 128 * (chunk // 2 + 1))

    def tiles_of(values):
        return [values[:, 128 * c : 128 * (c + 1)] for c in range(SPEC // 128)]

    def ready_halos(step, is_flow):
        if is_flow:
            for y in range(ROWS):
                flow_edges[step, 0, y : y + 1, :] = flows[step, COLS * y : COLS * y + 1, :]
                flow_edges[step, 1, y : y + 1, :] = flows[step, COLS * (y + 1) - 1 : COLS * (y + 1), :]
        else:
            for y in range(ROWS):
                edge_lines[0, y : y + 1, :] = waves[step, COLS * y : COLS * y + 1, :]
                edge_lines[1, y : y + 1, :] = waves[step, COLS * (y + 1) - 1 : COLS * (y + 1), :]
            places = (
                (wave_edges, 0, edge_lines[0], jnp.logical_not(goes_east)),
                (wave_edges, 1, edge_lines[1], goes_east),
                (band_edges, 0, waves[step, 0:COLS, :], jnp.logical_not(goes_north)),
                (band_edges, 1, waves[step, CELLS - COLS : CELLS, :], goes_north),
            )
            for edges, side, values, needed in places:
                for c, tile in enumerate(pack(tiles_of(values), needed)):
                    edges[step, side, :, 128 * c : 128 * (c + 1)] = tile

    def send_halos(step, is_flow, ready=False):
        if not ready:
            ready_halos(step, is_flow)
        for there, copy in halo_copies(step, is_flow):

            @pl.when(there)
            def _():
                copy().start()

    def receive_halos(step, is_flow):
        for k, halo in enumerate((flow_sides, flow_bands) if is_flow else (wave_sides, wave_bands)):
            both = halo.at[step]
            pltpu.make_async_copy(both, both, halo_recv.at[2 * step + is_flow, k]).wait()

    def pair_copy(index, k):
        peer = peers[k]
        return pltpu.make_async_remote_copy(
            src_ref=half_out.at[index - 1, peer] if index else outgoing.at[peer],
            dst_ref=half_in.at[index - 1, sec] if index else arrived.at[sec],
            send_sem=pair_send.at[index],
            recv_sem=pair_recv.at[index],
            device_id={"sec": peer},
            device_id_type=MESH,
        )

    def start_pairs(index):
        for k in range(sections - 1):
            pair_copy(index, k).start()

    def ready_first(message):
        outgoing[...] = message.reshape(sections, share, 128)
        arrived[sec] = outgoing[sec]

    def all_pairs(index):
        others = pl.ds(0, sections - 1)
        return pltpu.make_async_remote_copy(
            src_ref=half_out.at[index - 1, others] if index else outgoing.at[others],
            dst_ref=half_in.at[index - 1, others] if index else arrived.at[others],
            send_sem=pair_send.at[index],
            recv_sem=pair_recv.at[index],
            device_id={"sec": peers[0]},
            device_id_type=MESH,
        )

    def receive(index):
        all_pairs(index).wait_recv()

    def receive_first():
        receive(0)
        return arrived[...].reshape(CELLS, 128)

    def send_pairs(index, message):
        folded = jnp.where(low_half, message, pltpu.roll(message, CELLS - share // 2, 0))
        for k in range(sections):
            half_out[index - 1, k] = folded[share * k : share * k + share // 2, :]
        start_pairs(index)
        half_in[index - 1, sec] = half_out[index - 1, sec]

    def receive_pairs(index):
        receive(index)
        for k in range(sections):
            rows = half_in[index - 1, k]
            other = pltpu.roll(rows, 64, 1)
            unpacked[index - 1, share * k : share * k + share // 2, :] = jnp.where(low_rows, rows, other)
            unpacked[index - 1, share * k + share // 2 : share * (k + 1), :] = jnp.where(low_rows, other, rows)
        return unpacked[index - 1]

    def sent_halos(step, is_flow):
        for there, copy in halo_copies(step, is_flow):

            @pl.when(there)
            def _():
                copy().wait_send()

    def sent_pairs(index):
        all_pairs(index).wait_send()

    def stokes_part(values, chunk):
        high = values.astype(bf16)
        low = (values - high.astype(f32)).astype(bf16)
        both = jnp.concatenate([high, low], axis=0)
        return jnp.dot(both, stokes_table[256 * chunk : 256 * (chunk + 1), :], preferred_element_type=f32)

    def sorted_drift(step, drift):
        drift = drift[0:CELLS] + drift[CELLS:]
        drift = drift + pltpu.roll(drift, 64, 1)
        drifts[step] = drift
        high = round_half(drift)
        pieces = jnp.where(low_half, high, drift - high).astype(bf16)
        drift = jnp.dot(place, pieces, preferred_element_type=f32)
        return drift + pltpu.roll(drift, 64, 1)

    def neighbours(own, halos, step, y, lanes, chunk=None):
        bands_in, sides_in = halos
        rows = slice(COLS * y, COLS * (y + 1))
        here = own[step, rows, lanes]
        edge = lanes if chunk is None else half_lanes(chunk)
        fit = (lambda halo: halo) if chunk is None else (lambda halo: unpack(halo, chunk))
        west = fit(sides_in[step, 0, y : y + 1, edge])
        east = fit(sides_in[step, 1, y : y + 1, edge])
        return (
            here,
            jnp.where(first_column, west, pltpu.roll(here, 1, 0)),
            jnp.where(last_column, east, pltpu.roll(here, COLS - 1, 0)),
            own[step, COLS * (y - 1) : COLS * y, lanes] if y else fit(bands_in[step, 0, :, edge]),
            own[step, COLS * (y + 1) : COLS * (y + 2), lanes]
            if y < ROWS - 1
            else fit(bands_in[step, 1, :, edge]),
        )

    def find_spin(step):
        for y in range(ROWS):
            _, west, east, south, north = neighbours(flows, (flow_bands, flow_sides), step, y, slice(0, 128))
            sheared = jnp.where(zonal_row, south - north, east - west)
            spin = 0.5 * (sheared + pltpu.roll(sheared, 32, 1))
            spins[step, COLS * y : COLS * (y + 1), :] = spin + (0.2 + 0.6 * (global_row + y) / (ROWS * bands))

    def advect(step, grown=False):
        drift = None
        for chunk in range(SPEC // 128):
            lanes = slice(128 * chunk, 128 * (chunk + 1))
            stay = rates_ref[0:1, lanes]
            rate_x = rates_ref[1:2, lanes]
            rate_y = rates_ref[2:3, lanes]
            gain = rates_ref[3:4, lanes]
            for y in range(ROWS):
                rows = slice(COLS * y, COLS * (y + 1))
                here, west, east, south, north = neighbours(
                    waves, (wave_bands, wave_sides), step, y, lanes, chunk
                )
                moved = (
                    stay * here
                    + rate_x * jnp.where(goes_east, west, east)
                    + rate_y * jnp.where(goes_north, south, north)
                )
                behind = jnp.where(first_direction, pltpu.roll(moved, 97, 1), pltpu.roll(moved, 1, 1))
                forward = jnp.where(last_direction, pltpu.roll(moved, 31, 1), pltpu.roll(moved, 127, 1))
                beside = jnp.where(turn_sign[rows, :] > 0.0, behind, forward)
                rate = turn_size[rows, :] * gain
                moved = (moved + rate * (beside - moved)) * sea[rows, :]
                if grown:
                    waves[step + 1, rows, lanes] = moved * growths[rows, lanes]
                else:
                    turned[rows, lanes] = moved
            if grown and chunk % 2:
                part = stokes_part(waves[step + 1, :, 128 * (chunk - 1) : 128 * (chunk + 1)], chunk // 2)
                drift = part if drift is None else drift + part
        return drift

    def push(flow, spin, drift, wet):
        return (keep * wet) * (flow + twist * spin * pltpu.roll(flow + drift, 32, 1))

    def find_growth(seen):
        seen = jnp.concatenate([seen, seen[:, 0:64]], axis=1)
        for chunk in range(SPEC // 256):
            lanes = slice(256 * chunk, 256 * (chunk + 1))
            growths[:, lanes] = 1.0 + jnp.dot(seen, swell_table[:, lanes], preferred_element_type=f32)

    def grow(seen, step):
        seen = jnp.concatenate([seen, seen[:, 0:64]], axis=1)
        for chunk in range(SPEC // 256):
            lanes = slice(256 * chunk, 256 * (chunk + 1))
            growth = jnp.dot(seen, swell_table[:, lanes], preferred_element_type=f32)
            values = turned[:, lanes] * (1.0 + growth)
            if step == STEPS:
                spectra_out[:, lanes] = values
            else:
                waves[step, :, lanes] = values
        if step == STEPS:
            return None
        send_halos(step, 0)
        return find_drift(step)

    def find_drift(step):
        drift = None
        for chunk in range(SPEC // 256):
            part = stokes_part(waves[step, :, 256 * chunk : 256 * (chunk + 1)], chunk)
            drift = part if drift is None else drift + part
        return sorted_drift(step, drift)

    def first_seen(message):
        high = round_half(message)
        pieces = jnp.where(low_half, pltpu.roll(high, 64, 1), message - high).astype(bf16)
        seen = jnp.dot(place_back, pieces, preferred_element_type=f32)
        flow_at_waves[0] = seen + pltpu.roll(seen, 64, 1)
        return seen.astype(bf16)

    def next_seen(step, message):
        high = round_half(message)
        pieces = jnp.where(low_half, high, message - high).astype(bf16)
        both = jnp.dot(place_back, pieces, preferred_element_type=f32)
        both = both + pltpu.roll(both, 64, 1)
        other = pltpu.roll(both, 32, 1)
        spin = jnp.where(zonal, both, other)
        wet = jnp.where(zonal, other, both)
        flow = push(flow_at_waves[step - 1], spin, drifts[step - 1], wet)
        flow_at_waves[step] = flow
        high = round_half(flow)
        return jnp.where(low_half, high, flow - high).astype(bf16)

    def spin_message(step):
        return jnp.where(zonal, spins[step], sea[...])

    loads[4].wait()
    start_flow = currents_ref[...].reshape(CELLS, 2 * NDEPTH)
    flows[0] = jnp.concatenate([start_flow, start_flow], axis=1)
    for load in loads[5:]:
        load.wait()
    ready_halos(0, 1)
    ready_halos(0, 0)
    ready_first(jnp.where(low_half, find_drift(0), flows[0]))

    greeted = sections - 1 + has_south.astype(jnp.int32) + has_north.astype(jnp.int32)
    pl.semaphore_wait(barrier, greeted)

    start_pairs(0)
    send_halos(0, 1, ready=True)
    send_halos(0, 0, ready=True)

    receive_halos(0, 1)
    find_spin(0)
    send_pairs(1, spin_message(0))
    receive_halos(0, 0)
    advect(0)
    message = receive_first()
    flows[1] = push(flows[0], spins[0], jnp.where(low_half, message, pltpu.roll(message, 64, 1)), sea[...])
    send_halos(1, 1)
    send_pairs(2, grow(first_seen(message), 1))

    find_growth(next_seen(1, receive_pairs(1)))
    receive_halos(1, 1)
    find_spin(1)
    send_pairs(3, spin_message(1))
    receive_halos(1, 0)
    drift = advect(1, grown=True)
    send_halos(2, 0)
    send_pairs(4, sorted_drift(2, drift))
    flows[2] = push(flows[1], spins[1], receive_pairs(2), sea[...])
    send_halos(2, 1)

    for step in range(STEPS):
        sent_halos(step, 0)
        sent_halos(step, 1)
    for index in range(2 * STEPS - 1):
        sent_pairs(index)
    receive_halos(2, 0)
    advect(2)
    grow(next_seen(2, receive_pairs(3)), 3)
    receive_halos(2, 1)
    find_spin(2)
    currents_out[...] = push(flows[2], spins[2], receive_pairs(4), sea[...])[:, 0 : 2 * NDEPTH]


def store(waves_ref, flows_ref, waves_out, flows_out, sems):
    copies = [
        pltpu.make_async_copy(waves_ref, waves_out, sems.at[0]),
        pltpu.make_async_copy(flows_ref, flows_out, sems.at[1]),
    ]
    for copy in copies:
        copy.start()
    for copy in copies:
        copy.wait()


def solution(mesh):
    sections, bands = mesh.shape["sec"], mesh.shape["lat"]
    rates, stokes_table, swell_table = build_tables()
    share = CELLS // sections

    def per_device(spectra, turning, currents, drag_rates, land_mask, ocean_target):
        f32, bf16 = jnp.float32, jnp.bfloat16
        vmem = pl.BlockSpec(memory_space=pltpu.VMEM)
        hbm = pl.BlockSpec(memory_space=pltpu.HBM)
        operands = (
            spectra.reshape(CELLS, SPEC),
            turning,
            currents,
            drag_rates.reshape(1, NDEPTH),
            land_mask,
            ocean_target,
            jnp.asarray(rates),
            jnp.asarray(stokes_table),
            jnp.asarray(swell_table),
        )
        waves, flows = pl.pallas_call(
            lambda *refs: kernel(sections, bands, *refs),
            out_shape=(
                jax.ShapeDtypeStruct((CELLS, SPEC), f32),
                jax.ShapeDtypeStruct((CELLS, 2 * NDEPTH), f32),
            ),
            in_specs=[hbm] * 9,
            out_specs=(vmem, vmem),
            scratch_shapes=[
                pltpu.VMEM((STEPS, CELLS, SPEC), f32),
                pltpu.VMEM((STEPS, CELLS, 128), f32),
                pltpu.VMEM((STEPS, 2, COLS, SPEC // 2), f32),
                pltpu.VMEM((STEPS, 2, ROWS, SPEC // 2), f32),
                pltpu.VMEM((STEPS, 2, COLS, 128), f32),
                pltpu.VMEM((STEPS, 2, ROWS, 128), f32),
                pltpu.VMEM((STEPS, 2, ROWS, SPEC // 2), f32),
                pltpu.VMEM((STEPS, 2, ROWS, 128), f32),
                pltpu.VMEM((sections, share, 128), f32),
                pltpu.VMEM((sections, share, 128), f32),
                pltpu.VMEM((2 * STEPS - 2, sections, share // 2, 128), f32),
                pltpu.VMEM((2 * STEPS - 2, sections, share // 2, 128), f32),
                pltpu.VMEM((2 * STEPS - 2, CELLS, 128), f32),
                pltpu.VMEM((2, ROWS, SPEC), f32),
                pltpu.VMEM((STEPS, 2, COLS, SPEC // 2), f32),
                pltpu.VMEM((COLS, SPEC // 2), f32),
                pltpu.VMEM((ROWS, SPEC // 2), f32),
                pltpu.VMEM((CELLS, SPEC), f32),
                pltpu.VMEM((CELLS, SPEC), f32),
                pltpu.VMEM((STEPS, CELLS, 128), f32),
                pltpu.VMEM((STEPS, CELLS, 128), f32),
                pltpu.VMEM((STEPS, CELLS, 128), f32),
                pltpu.VMEM((ROWS, COLS), f32),
                pltpu.VMEM((ROWS, COLS, 2 * NDEPTH), f32),
                pltpu.VMEM((1, NDEPTH), f32),
                pltpu.VMEM((ROWS, COLS), jnp.int32),
                pltpu.VMEM((ROWS, COLS), jnp.int32),
                pltpu.VMEM((8, SPEC), f32),
                pltpu.VMEM((SPEC, 128), bf16),
                pltpu.VMEM((6 * NDEPTH, SPEC), bf16),
                pltpu.VMEM((4, 8, 128), f32),
                pltpu.VMEM((CELLS, 128), f32),
                pltpu.VMEM((CELLS, 128), f32),
                pltpu.VMEM((CELLS, 128), f32),
                pltpu.SemaphoreType.DMA((9,)),
                pltpu.SemaphoreType.DMA((2 * STEPS, 4)),
                pltpu.SemaphoreType.DMA((2 * STEPS, 2)),
                pltpu.SemaphoreType.DMA((2 * STEPS - 1,)),
                pltpu.SemaphoreType.DMA((2 * STEPS - 1,)),
            ],
            compiler_params=pltpu.CompilerParams(
                collective_id=0, has_side_effects=True, vmem_limit_bytes=24 << 20
            ),
        )(*[pltpu.with_memory_space_constraint(x, pltpu.HBM) for x in operands])
        waves, flows = pl.pallas_call(
            store,
            out_shape=(
                jax.ShapeDtypeStruct((CELLS, SPEC), f32),
                jax.ShapeDtypeStruct((CELLS, 2 * NDEPTH), f32),
            ),
            in_specs=[vmem, vmem],
            out_specs=(hbm, hbm),
            scratch_shapes=[pltpu.SemaphoreType.DMA((2,))],
        )(*[pltpu.with_memory_space_constraint(x, pltpu.VMEM) for x in (waves, flows)])
        return waves.reshape(ROWS, COLS, SPEC), flows.reshape(ROWS, COLS, 2 * NDEPTH)

    return jax.shard_map(
        per_device,
        mesh=mesh,
        in_specs=(
            P("lat", "sec", None),
            P("lat", "sec"),
            P("lat", "sec", None),
            P(),
            P("lat", "sec"),
            P("lat", "sec"),
        ),
        out_specs=(P("lat", "sec", None), P("lat", "sec", None)),
        check_vma=False,
    )
```

```python
import math

import jax
import jax.numpy as jnp
import ml_dtypes
import numpy as np
from jax import lax
from jax.experimental import pallas as pl
from jax.experimental.pallas import tpu as pltpu
from jax.sharding import PartitionSpec as P

NFREQ = 24
NDIR = 32
NDEPTH = 32
STEPS = 3
ROWS = 4
COLS = 24
CELLS = ROWS * COLS
SPEC = NFREQ * NDIR
RING = 3
SIDES, BANDS = slice(0, 2), slice(2, 4)

STOKES_SCALE = 0.1
OCEAN_DT = 0.3
CURRENT_GAIN = 0.2

MESH = pl.DeviceIdType.MESH


def halves(table):
    high = table.astype(ml_dtypes.bfloat16)
    low = (table - high.astype(np.float32)).astype(ml_dtypes.bfloat16)
    return high, low


def build_tables():
    f32 = np.float32
    fraction = np.arange(NFREQ, dtype=f32) / f32(NFREQ - 1)
    angles = (np.arange(NDIR, dtype=f32) + f32(0.5)) * f32(2.0 * math.pi / NDIR)
    east = np.cos(angles).astype(f32)
    north = np.sin(angles).astype(f32)
    compass = np.stack([east, north])
    courant = f32(0.1) + f32(0.3) * fraction
    depth_level = f32(0.5) + f32(NDEPTH - 2) * (f32(1.0) - fraction)
    levels = np.arange(NDEPTH, dtype=f32)
    weights = np.maximum(f32(1.0) - np.abs(levels[None, :] - depth_level[:, None]), f32(0.0))
    mean_weights = weights / np.sum(weights, axis=1, keepdims=True)
    x_rate = (courant[:, None] * east[None, :]).reshape(-1)
    y_rate = (courant[:, None] * north[None, :]).reshape(-1)
    turn_gain = f32(1.0) - f32(0.5) * fraction
    growth = f32(CURRENT_GAIN) * (f32(1.0) + fraction)
    stokes = (
        f32(STOKES_SCALE) * weights[:, None, None, :] * compass.T[None, :, :, None]
    ).reshape(SPEC, 2 * NDEPTH)
    swell = (
        growth[None, None, :, None] * mean_weights.T[None, :, :, None] * compass[:, None, None, :]
    ).reshape(2 * NDEPTH, SPEC)
    rates = np.zeros((8, SPEC), f32)
    rates[0] = f32(1.0) - np.abs(x_rate) - np.abs(y_rate)
    rates[1] = np.abs(x_rate)
    rates[2] = np.abs(y_rate)
    rates[3] = np.repeat(turn_gain, NDIR)
    stokes_table = np.concatenate(halves(stokes), axis=1)
    swell_high, swell_low = halves(swell)
    swell_table = np.concatenate([swell_high, swell_high, swell_low], axis=0)
    return rates, stokes_table, swell_table


def iota(shape, dim):
    return lax.broadcasted_iota(jnp.int32, shape, dim)


def round_half(x):
    return x.astype(jnp.bfloat16).astype(jnp.float32)


def kernel(
    sections,
    bands,
    spectra_hbm,
    turning_hbm,
    currents_hbm,
    drag_hbm,
    land_hbm,
    target_hbm,
    rates_hbm,
    stokes_hbm,
    swell_hbm,
    spectra_out,
    currents_out,
    waves,
    flows,
    wave_bands,
    wave_sides,
    flow_bands,
    flow_sides,
    wave_edges,
    flow_edges,
    outgoing,
    arrived,
    half_out,
    half_in,
    unpacked,
    edge_lines,
    band_edges,
    zeros,
    no_side,
    turned,
    growths,
    spins,
    drifts,
    flow_at_waves,
    turning_ref,
    currents_ref,
    drag_ref,
    land_ref,
    target_ref,
    rates_ref,
    stokes_table,
    swell_table,
    tiny,
    turn_size,
    turn_sign,
    sea,
    load_sem,
    halo_send,
    halo_recv,
    pair_send,
    pair_recv,
):
    f32, bf16 = jnp.float32, jnp.bfloat16
    share = CELLS // sections
    sec = lax.axis_index("sec")
    lat = lax.axis_index("lat")
    has_west, has_east = sec > 0, sec < sections - 1
    has_south, has_north = lat > 0, lat < bands - 1

    lines = sections // RING
    line, spot = lax.div(sec, RING), lax.rem(sec, RING)
    hops = sorted(
        ((over, along) for over in range(lines) for along in range(RING) if over or along),
        key=lambda hop: (hop[1] == 0, -min(hop[0], lines - hop[0])),
    )

    def peer_of(hop):
        far, near = line + hop[0], spot + hop[1]
        far = jnp.where(far >= lines, far - lines, far)
        return RING * far + jnp.where(near >= RING, near - RING, near)

    peers = [peer_of(hop) for hop in hops]

    barrier = pltpu.get_barrier_semaphore()
    for peer in peers:
        pl.semaphore_signal(barrier, inc=1, device_id={"sec": peer}, device_id_type=MESH)

    for there, other in ((has_south, lat - 1), (has_north, lat + 1)):

        @pl.when(there)
        def _():
            pl.semaphore_signal(barrier, inc=1, device_id={"lat": other}, device_id_type=MESH)

    pairs = (
        (turning_hbm, turning_ref),
        (drag_hbm, drag_ref),
        (land_hbm, land_ref),
        (target_hbm, target_ref),
        (currents_hbm, currents_ref),
        (rates_hbm, rates_ref),
        (spectra_hbm, waves.at[0]),
        (stokes_hbm, stokes_table),
        (swell_hbm, swell_table),
    )
    loads = [pltpu.make_async_copy(there, here, load_sem.at[i]) for i, (there, here) in enumerate(pairs)]
    for load in loads:
        load.start()

    zeros[...] = jnp.zeros_like(zeros)
    no_side[...] = jnp.zeros_like(no_side)
    for step in range(STEPS):
        for kind, (bands_in, sides_in) in enumerate(((wave_bands, wave_sides), (flow_bands, flow_sides))):
            width = bands_in.shape[-1]
            for there, halo, k in (
                (has_west, sides_in.at[step, 0], 0),
                (has_east, sides_in.at[step, 1], 0),
                (has_south, bands_in.at[step, 0], 1),
                (has_north, bands_in.at[step, 1], 1),
            ):

                @pl.when(jnp.logical_not(there))
                def _():
                    empty = zeros.at[pl.ds(0, COLS), pl.ds(0, width)] if k else no_side.at[:, pl.ds(0, width)]
                    pltpu.make_async_copy(empty, halo, halo_recv.at[2 * step + kind, k]).start()

    tiny[...] = jnp.zeros_like(tiny)
    for load in loads[:4]:
        load.wait()
    tiny[0, 0:ROWS, 0:COLS] = turning_ref[...]
    tiny[1, 0:ROWS, 0:COLS] = land_ref[...].astype(f32)
    tiny[2, 0:ROWS, 0:COLS] = target_ref[...].astype(f32)
    tiny[3, 0:1, 0:NDEPTH] = 1.0 - drag_ref[...]

    lane_row = iota((1, 128), 1)
    target_rows = tiny[2]
    targets = jnp.full((1, 128), 99.0, f32)
    for y in range(ROWS):
        row = target_rows[y : y + 1, :]
        moved = pltpu.roll(row, COLS * y, 1) if y else row
        inside = jnp.logical_and(lane_row >= COLS * y, lane_row < COLS * (y + 1))
        targets = jnp.where(inside, moved, targets)
    matches = (iota((16, 128), 0).astype(f32) == targets).astype(f32)
    earlier = (iota((128, 128), 0) < iota((128, 128), 1)).astype(f32)
    before = jnp.dot(matches.astype(bf16), earlier.astype(bf16), preferred_element_type=f32)
    rank = jnp.sum(matches * before, axis=0, keepdims=True)
    place_of = targets * share + rank
    place = (iota((128, 128), 0).astype(f32) == place_of).astype(f32)
    place_back = jnp.transpose(place)[0:CELLS, 0:CELLS].astype(bf16)
    place = place[0:CELLS, 0:CELLS].astype(bf16)

    turn_columns = jnp.transpose(tiny[0])
    sea_columns = jnp.transpose(tiny[1])
    for y in range(ROWS):
        rows = slice(COLS * y, COLS * (y + 1))
        turn = jnp.broadcast_to(turn_columns[0:COLS, y : y + 1], (COLS, 128))
        turn_size[rows, :] = jnp.abs(turn)
        turn_sign[rows, :] = turn
        sea[rows, :] = jnp.broadcast_to(sea_columns[0:COLS, y : y + 1], (COLS, 128))

    keep = tiny[3, 0:1, :]
    keep = keep + pltpu.roll(keep, 32, 1)
    keep = keep + pltpu.roll(keep, 64, 1)

    lane = iota((COLS, 128), 1)
    column = iota((COLS, 128), 0)
    first_column = column == 0
    last_column = column == COLS - 1
    direction = lane & (NDIR - 1)
    goes_east = jnp.logical_or(direction < NDIR // 4, direction >= 3 * NDIR // 4)
    goes_north = direction < NDIR // 2
    first_direction = direction == 0
    last_direction = direction == NDIR - 1
    full_lane = iota((CELLS, 128), 1)
    low_half = full_lane < 64
    zonal = (full_lane & 63) < 32
    low_rows = iota((share // 2, 128), 1) < 64
    zonal_row = (lane & 63) < 32
    twist = jnp.where(zonal, OCEAN_DT, -OCEAN_DT)
    global_row = (lat * ROWS).astype(f32)

    def halo_copies(step, is_flow):
        bands_in, sides_in = (flow_bands, flow_sides) if is_flow else (wave_bands, wave_sides)
        edges = (flow_edges if is_flow else wave_edges).at[step]
        if is_flow:
            first = flows.at[step, pl.ds(0, COLS)]
            final = flows.at[step, pl.ds(CELLS - COLS, COLS)]
        else:
            first, final = band_edges.at[step, 0], band_edges.at[step, 1]
        index = 2 * step + is_flow
        plan = (
            (has_west, edges.at[0], sides_in.at[step, 1], 0, {"sec": sec - 1}),
            (has_east, edges.at[1], sides_in.at[step, 0], 0, {"sec": sec + 1}),
            (has_south, first, bands_in.at[step, 1], 1, {"lat": lat - 1}),
            (has_north, final, bands_in.at[step, 0], 1, {"lat": lat + 1}),
        )
        for number, (there, source, halo, k, device) in enumerate(plan):
            yield there, lambda source=source, halo=halo, device=device, k=k, number=number: pltpu.make_async_remote_copy(
                src_ref=source,
                dst_ref=halo,
                send_sem=halo_send.at[index, number],
                recv_sem=halo_recv.at[index, k],
                device_id=device,
                device_id_type=MESH,
            )

    def pack(tiles, needed):
        return [
            jnp.where(needed[0 : tiles[0].shape[0]], tiles[2 * c], pltpu.roll(tiles[2 * c + 1], 16, 1))
            for c in range(SPEC // 256)
        ]

    def unpack(halo, chunk):
        return pltpu.roll(halo, 112, 1) if chunk % 2 else halo

    def half_lanes(chunk):
        return slice(128 * (chunk // 2), 128 * (chunk // 2 + 1))

    def tiles_of(values):
        return [values[:, 128 * c : 128 * (c + 1)] for c in range(SPEC // 128)]

    def ready_sides(step, is_flow):
        if is_flow:
            for y in range(ROWS):
                flow_edges[step, 0, y : y + 1, :] = flows[step, COLS * y : COLS * y + 1, :]
                flow_edges[step, 1, y : y + 1, :] = flows[step, COLS * (y + 1) - 1 : COLS * (y + 1), :]
        else:
            for y in range(ROWS):
                edge_lines[0, y : y + 1, :] = waves[step, COLS * y : COLS * y + 1, :]
                edge_lines[1, y : y + 1, :] = waves[step, COLS * (y + 1) - 1 : COLS * (y + 1), :]
            for side, needed in ((0, jnp.logical_not(goes_east)), (1, goes_east)):
                for c, tile in enumerate(pack(tiles_of(edge_lines[side]), needed)):
                    wave_edges[step, side, :, 128 * c : 128 * (c + 1)] = tile

    def ready_bands(step, is_flow):
        if not is_flow:
            for side, needed in ((0, jnp.logical_not(goes_north)), (1, goes_north)):
                rows = slice(side * (CELLS - COLS), side * (CELLS - COLS) + COLS)
                for c, tile in enumerate(pack(tiles_of(waves[step, rows, :]), needed)):
                    band_edges[step, side, :, 128 * c : 128 * (c + 1)] = tile

    def ready_halos(step, is_flow):
        ready_sides(step, is_flow)
        ready_bands(step, is_flow)

    def start_halos(step, is_flow, part):
        for sends, copy in list(halo_copies(step, is_flow))[part]:

            @pl.when(sends)
            def _():
                copy().start()

    def send_halos(step, is_flow, ready=False):
        if not ready:
            ready_sides(step, is_flow)
        start_halos(step, is_flow, SIDES)
        if not ready:
            ready_bands(step, is_flow)
        start_halos(step, is_flow, BANDS)

    def receive_halos(step, is_flow):
        for k, halo in enumerate((flow_sides, flow_bands) if is_flow else (wave_sides, wave_bands)):
            both = halo.at[step]
            pltpu.make_async_copy(both, both, halo_recv.at[2 * step + is_flow, k]).wait()

    def pair_copy(index, k):
        peer = peers[k]
        return pltpu.make_async_remote_copy(
            src_ref=half_out.at[index - 1, peer] if index else outgoing.at[peer],
            dst_ref=half_in.at[index - 1, sec] if index else arrived.at[sec],
            send_sem=pair_send.at[index],
            recv_sem=pair_recv.at[index],
            device_id={"sec": peer},
            device_id_type=MESH,
        )

    far, near = range(sections - lines), range(sections - lines, sections - 1)

    def start_pairs(index, which=None):
        for k in range(sections - 1) if which is None else which:
            pair_copy(index, k).start()

    def ready_first(message):
        outgoing[...] = message.reshape(sections, share, 128)
        arrived[sec] = outgoing[sec]

    def all_pairs(index):
        others = pl.ds(0, sections - 1)
        return pltpu.make_async_remote_copy(
            src_ref=half_out.at[index - 1, others] if index else outgoing.at[others],
            dst_ref=half_in.at[index - 1, others] if index else arrived.at[others],
            send_sem=pair_send.at[index],
            recv_sem=pair_recv.at[index],
            device_id={"sec": peers[0]},
            device_id_type=MESH,
        )

    def receive(index):
        all_pairs(index).wait_recv()

    def receive_first():
        receive(0)
        return arrived[...].reshape(CELLS, 128)

    def send_pairs(index, message, which=None):
        folded = jnp.where(low_half, message, pltpu.roll(message, CELLS - share // 2, 0))
        for k in range(sections):
            half_out[index - 1, k] = folded[share * k : share * k + share // 2, :]
        start_pairs(index, which)
        half_in[index - 1, sec] = half_out[index - 1, sec]

    def receive_pairs(index):
        receive(index)
        for k in range(sections):
            rows = half_in[index - 1, k]
            other = pltpu.roll(rows, 64, 1)
            unpacked[index - 1, share * k : share * k + share // 2, :] = jnp.where(low_rows, rows, other)
            unpacked[index - 1, share * k + share // 2 : share * (k + 1), :] = jnp.where(low_rows, other, rows)
        return unpacked[index - 1]

    def sent_halos(step, is_flow):
        for there, copy in halo_copies(step, is_flow):

            @pl.when(there)
            def _():
                copy().wait_send()

    def sent_pairs(index):
        all_pairs(index).wait_send()

    def stokes_part(values, chunk):
        high = values.astype(bf16)
        low = (values - high.astype(f32)).astype(bf16)
        both = jnp.concatenate([high, low], axis=0)
        return jnp.dot(both, stokes_table[256 * chunk : 256 * (chunk + 1), :], preferred_element_type=f32)

    def sorted_drift(step, drift):
        drift = drift[0:CELLS] + drift[CELLS:]
        drift = drift + pltpu.roll(drift, 64, 1)
        drifts[step] = drift
        high = round_half(drift)
        pieces = jnp.where(low_half, high, drift - high).astype(bf16)
        drift = jnp.dot(place, pieces, preferred_element_type=f32)
        return drift + pltpu.roll(drift, 64, 1)

    def neighbours(own, halos, step, y, lanes, chunk=None):
        bands_in, sides_in = halos
        rows = slice(COLS * y, COLS * (y + 1))
        here = own[step, rows, lanes]
        edge = lanes if chunk is None else half_lanes(chunk)
        fit = (lambda halo: halo) if chunk is None else (lambda halo: unpack(halo, chunk))
        west = fit(sides_in[step, 0, y : y + 1, edge])
        east = fit(sides_in[step, 1, y : y + 1, edge])
        return (
            here,
            jnp.where(first_column, west, pltpu.roll(here, 1, 0)),
            jnp.where(last_column, east, pltpu.roll(here, COLS - 1, 0)),
            own[step, COLS * (y - 1) : COLS * y, lanes] if y else fit(bands_in[step, 0, :, edge]),
            own[step, COLS * (y + 1) : COLS * (y + 2), lanes]
            if y < ROWS - 1
            else fit(bands_in[step, 1, :, edge]),
        )

    def find_spin(step):
        for y in range(ROWS):
            _, west, east, south, north = neighbours(flows, (flow_bands, flow_sides), step, y, slice(0, 128))
            sheared = jnp.where(zonal_row, south - north, east - west)
            spin = 0.5 * (sheared + pltpu.roll(sheared, 32, 1))
            spins[step, COLS * y : COLS * (y + 1), :] = spin + (0.2 + 0.6 * (global_row + y) / (ROWS * bands))

    def advect(step, grown=False):
        drift = None
        for chunk in range(SPEC // 128):
            lanes = slice(128 * chunk, 128 * (chunk + 1))
            stay = rates_ref[0:1, lanes]
            rate_x = rates_ref[1:2, lanes]
            rate_y = rates_ref[2:3, lanes]
            gain = rates_ref[3:4, lanes]
            for y in range(ROWS):
                rows = slice(COLS * y, COLS * (y + 1))
                here, west, east, south, north = neighbours(
                    waves, (wave_bands, wave_sides), step, y, lanes, chunk
                )
                moved = (
                    stay * here
                    + rate_x * jnp.where(goes_east, west, east)
                    + rate_y * jnp.where(goes_north, south, north)
                )
                behind = jnp.where(first_direction, pltpu.roll(moved, 97, 1), pltpu.roll(moved, 1, 1))
                forward = jnp.where(last_direction, pltpu.roll(moved, 31, 1), pltpu.roll(moved, 127, 1))
                beside = jnp.where(turn_sign[rows, :] > 0.0, behind, forward)
                rate = turn_size[rows, :] * gain
                moved = (moved + rate * (beside - moved)) * sea[rows, :]
                if grown:
                    waves[step + 1, rows, lanes] = moved * growths[rows, lanes]
                else:
                    turned[rows, lanes] = moved
            if grown and chunk % 2:
                part = stokes_part(waves[step + 1, :, 128 * (chunk - 1) : 128 * (chunk + 1)], chunk // 2)
                drift = part if drift is None else drift + part
        return drift

    def push(flow, spin, drift, wet):
        return (keep * wet) * (flow + twist * spin * pltpu.roll(flow + drift, 32, 1))

    def find_growth(seen):
        seen = jnp.concatenate([seen, seen[:, 0:64]], axis=1)
        for chunk in range(SPEC // 256):
            lanes = slice(256 * chunk, 256 * (chunk + 1))
            growths[:, lanes] = 1.0 + jnp.dot(seen, swell_table[:, lanes], preferred_element_type=f32)

    def grow(seen, step):
        seen = jnp.concatenate([seen, seen[:, 0:64]], axis=1)
        for chunk in range(SPEC // 256):
            lanes = slice(256 * chunk, 256 * (chunk + 1))
            growth = jnp.dot(seen, swell_table[:, lanes], preferred_element_type=f32)
            values = turned[:, lanes] * (1.0 + growth)
            if step == STEPS:
                spectra_out[:, lanes] = values
            else:
                waves[step, :, lanes] = values
        if step == STEPS:
            return None
        send_halos(step, 0)
        return find_drift(step)

    def find_drift(step):
        drift = None
        for chunk in range(SPEC // 256):
            part = stokes_part(waves[step, :, 256 * chunk : 256 * (chunk + 1)], chunk)
            drift = part if drift is None else drift + part
        return sorted_drift(step, drift)

    def first_seen(message):
        high = round_half(message)
        pieces = jnp.where(low_half, pltpu.roll(high, 64, 1), message - high).astype(bf16)
        seen = jnp.dot(place_back, pieces, preferred_element_type=f32)
        flow_at_waves[0] = seen + pltpu.roll(seen, 64, 1)
        return seen.astype(bf16)

    def next_seen(step, message):
        high = round_half(message)
        pieces = jnp.where(low_half, high, message - high).astype(bf16)
        both = jnp.dot(place_back, pieces, preferred_element_type=f32)
        both = both + pltpu.roll(both, 64, 1)
        other = pltpu.roll(both, 32, 1)
        spin = jnp.where(zonal, both, other)
        wet = jnp.where(zonal, other, both)
        flow = push(flow_at_waves[step - 1], spin, drifts[step - 1], wet)
        flow_at_waves[step] = flow
        high = round_half(flow)
        return jnp.where(low_half, high, flow - high).astype(bf16)

    def spin_message(step):
        return jnp.where(zonal, spins[step], sea[...])

    loads[4].wait()
    start_flow = currents_ref[...].reshape(CELLS, 2 * NDEPTH)
    flows[0] = jnp.concatenate([start_flow, start_flow], axis=1)
    for load in loads[5:]:
        load.wait()
    ready_halos(0, 1)
    ready_halos(0, 0)
    ready_first(jnp.where(low_half, find_drift(0), flows[0]))

    greeted = sections - 1 + has_south.astype(jnp.int32) + has_north.astype(jnp.int32)
    pl.semaphore_wait(barrier, greeted)

    start_pairs(0, far)
    start_halos(0, 1, SIDES)
    start_halos(0, 0, SIDES)
    start_pairs(0, near)
    start_halos(0, 1, BANDS)
    start_halos(0, 0, BANDS)

    receive_halos(0, 1)
    find_spin(0)
    send_pairs(1, spin_message(0))
    receive_halos(0, 0)
    advect(0)
    message = receive_first()
    flows[1] = push(flows[0], spins[0], jnp.where(low_half, message, pltpu.roll(message, 64, 1)), sea[...])
    send_halos(1, 1)
    send_pairs(2, grow(first_seen(message), 1))

    find_growth(next_seen(1, receive_pairs(1)))
    receive_halos(1, 1)
    find_spin(1)
    send_pairs(3, spin_message(1), far)
    receive_halos(1, 0)
    drift = advect(1, grown=True)
    send_halos(2, 0)
    start_pairs(3, near)
    send_pairs(4, sorted_drift(2, drift))
    flows[2] = push(flows[1], spins[1], receive_pairs(2), sea[...])
    send_halos(2, 1)

    for step in range(STEPS):
        sent_halos(step, 0)
        sent_halos(step, 1)
    for index in range(2 * STEPS - 1):
        sent_pairs(index)
    receive_halos(2, 0)
    advect(2)
    grow(next_seen(2, receive_pairs(3)), 3)
    receive_halos(2, 1)
    find_spin(2)
    currents_out[...] = push(flows[2], spins[2], receive_pairs(4), sea[...])[:, 0 : 2 * NDEPTH]


def store(waves_ref, flows_ref, waves_out, flows_out, sems):
    copies = [
        pltpu.make_async_copy(waves_ref, waves_out, sems.at[0]),
        pltpu.make_async_copy(flows_ref, flows_out, sems.at[1]),
    ]
    for copy in copies:
        copy.start()
    for copy in copies:
        copy.wait()


def solution(mesh):
    sections, bands = mesh.shape["sec"], mesh.shape["lat"]
    rates, stokes_table, swell_table = build_tables()
    share = CELLS // sections

    def per_device(spectra, turning, currents, drag_rates, land_mask, ocean_target):
        f32, bf16 = jnp.float32, jnp.bfloat16
        vmem = pl.BlockSpec(memory_space=pltpu.VMEM)
        hbm = pl.BlockSpec(memory_space=pltpu.HBM)
        operands = (
            spectra.reshape(CELLS, SPEC),
            turning,
            currents,
            drag_rates.reshape(1, NDEPTH),
            land_mask,
            ocean_target,
            jnp.asarray(rates),
            jnp.asarray(stokes_table),
            jnp.asarray(swell_table),
        )
        waves, flows = pl.pallas_call(
            lambda *refs: kernel(sections, bands, *refs),
            out_shape=(
                jax.ShapeDtypeStruct((CELLS, SPEC), f32),
                jax.ShapeDtypeStruct((CELLS, 2 * NDEPTH), f32),
            ),
            in_specs=[hbm] * 9,
            out_specs=(vmem, vmem),
            scratch_shapes=[
                pltpu.VMEM((STEPS, CELLS, SPEC), f32),
                pltpu.VMEM((STEPS, CELLS, 128), f32),
                pltpu.VMEM((STEPS, 2, COLS, SPEC // 2), f32),
                pltpu.VMEM((STEPS, 2, ROWS, SPEC // 2), f32),
                pltpu.VMEM((STEPS, 2, COLS, 128), f32),
                pltpu.VMEM((STEPS, 2, ROWS, 128), f32),
                pltpu.VMEM((STEPS, 2, ROWS, SPEC // 2), f32),
                pltpu.VMEM((STEPS, 2, ROWS, 128), f32),
                pltpu.VMEM((sections, share, 128), f32),
                pltpu.VMEM((sections, share, 128), f32),
                pltpu.VMEM((2 * STEPS - 2, sections, share // 2, 128), f32),
                pltpu.VMEM((2 * STEPS - 2, sections, share // 2, 128), f32),
                pltpu.VMEM((2 * STEPS - 2, CELLS, 128), f32),
                pltpu.VMEM((2, ROWS, SPEC), f32),
                pltpu.VMEM((STEPS, 2, COLS, SPEC // 2), f32),
                pltpu.VMEM((COLS, SPEC // 2), f32),
                pltpu.VMEM((ROWS, SPEC // 2), f32),
                pltpu.VMEM((CELLS, SPEC), f32),
                pltpu.VMEM((CELLS, SPEC), f32),
                pltpu.VMEM((STEPS, CELLS, 128), f32),
                pltpu.VMEM((STEPS, CELLS, 128), f32),
                pltpu.VMEM((STEPS, CELLS, 128), f32),
                pltpu.VMEM((ROWS, COLS), f32),
                pltpu.VMEM((ROWS, COLS, 2 * NDEPTH), f32),
                pltpu.VMEM((1, NDEPTH), f32),
                pltpu.VMEM((ROWS, COLS), jnp.int32),
                pltpu.VMEM((ROWS, COLS), jnp.int32),
                pltpu.VMEM((8, SPEC), f32),
                pltpu.VMEM((SPEC, 128), bf16),
                pltpu.VMEM((6 * NDEPTH, SPEC), bf16),
                pltpu.VMEM((4, 8, 128), f32),
                pltpu.VMEM((CELLS, 128), f32),
                pltpu.VMEM((CELLS, 128), f32),
                pltpu.VMEM((CELLS, 128), f32),
                pltpu.SemaphoreType.DMA((9,)),
                pltpu.SemaphoreType.DMA((2 * STEPS, 4)),
                pltpu.SemaphoreType.DMA((2 * STEPS, 2)),
                pltpu.SemaphoreType.DMA((2 * STEPS - 1,)),
                pltpu.SemaphoreType.DMA((2 * STEPS - 1,)),
            ],
            compiler_params=pltpu.CompilerParams(
                collective_id=0, has_side_effects=True, vmem_limit_bytes=24 << 20
            ),
        )(*[pltpu.with_memory_space_constraint(x, pltpu.HBM) for x in operands])
        waves, flows = pl.pallas_call(
            store,
            out_shape=(
                jax.ShapeDtypeStruct((CELLS, SPEC), f32),
                jax.ShapeDtypeStruct((CELLS, 2 * NDEPTH), f32),
            ),
            in_specs=[vmem, vmem],
            out_specs=(hbm, hbm),
            scratch_shapes=[pltpu.SemaphoreType.DMA((2,))],
        )(*[pltpu.with_memory_space_constraint(x, pltpu.VMEM) for x in (waves, flows)])
        return waves.reshape(ROWS, COLS, SPEC), flows.reshape(ROWS, COLS, 2 * NDEPTH)

    return jax.shard_map(
        per_device,
        mesh=mesh,
        in_specs=(
            P("lat", "sec", None),
            P("lat", "sec"),
            P("lat", "sec", None),
            P(),
            P("lat", "sec"),
            P("lat", "sec"),
        ),
        out_specs=(P("lat", "sec", None), P("lat", "sec", None)),
        check_vma=False,
    )
```

```python
import math

import jax
import jax.numpy as jnp
import ml_dtypes
import numpy as np
from jax import lax
from jax.experimental import pallas as pl
from jax.experimental.pallas import tpu as pltpu
from jax.sharding import PartitionSpec as P

NFREQ = 24
NDIR = 32
NDEPTH = 32
STEPS = 3
ROWS = 4
COLS = 24
CELLS = ROWS * COLS
SPEC = NFREQ * NDIR
RING = 3

STOKES_SCALE = 0.1
OCEAN_DT = 0.3
CURRENT_GAIN = 0.2

MESH = pl.DeviceIdType.MESH


def halves(table):
    high = table.astype(ml_dtypes.bfloat16)
    low = (table - high.astype(np.float32)).astype(ml_dtypes.bfloat16)
    return high, low


def build_tables():
    f32 = np.float32
    fraction = np.arange(NFREQ, dtype=f32) / f32(NFREQ - 1)
    angles = (np.arange(NDIR, dtype=f32) + f32(0.5)) * f32(2.0 * math.pi / NDIR)
    east = np.cos(angles).astype(f32)
    north = np.sin(angles).astype(f32)
    compass = np.stack([east, north])
    courant = f32(0.1) + f32(0.3) * fraction
    depth_level = f32(0.5) + f32(NDEPTH - 2) * (f32(1.0) - fraction)
    levels = np.arange(NDEPTH, dtype=f32)
    weights = np.maximum(f32(1.0) - np.abs(levels[None, :] - depth_level[:, None]), f32(0.0))
    mean_weights = weights / np.sum(weights, axis=1, keepdims=True)
    x_rate = (courant[:, None] * east[None, :]).reshape(-1)
    y_rate = (courant[:, None] * north[None, :]).reshape(-1)
    turn_gain = f32(1.0) - f32(0.5) * fraction
    growth = f32(CURRENT_GAIN) * (f32(1.0) + fraction)
    stokes = (
        f32(STOKES_SCALE) * weights[:, None, None, :] * compass.T[None, :, :, None]
    ).reshape(SPEC, 2 * NDEPTH)
    swell = (
        growth[None, None, :, None] * mean_weights.T[None, :, :, None] * compass[:, None, None, :]
    ).reshape(2 * NDEPTH, SPEC)
    rates = np.zeros((8, SPEC), f32)
    rates[0] = f32(1.0) - np.abs(x_rate) - np.abs(y_rate)
    rates[1] = np.abs(x_rate)
    rates[2] = np.abs(y_rate)
    rates[3] = np.repeat(turn_gain, NDIR)
    stokes_table = np.concatenate(halves(stokes), axis=1)
    swell_high, swell_low = halves(swell)
    swell_table = np.concatenate([swell_high, swell_high, swell_low], axis=0)
    return rates, stokes_table, swell_table


def iota(shape, dim):
    return lax.broadcasted_iota(jnp.int32, shape, dim)


def round_half(x):
    return x.astype(jnp.bfloat16).astype(jnp.float32)


def kernel(
    sections,
    bands,
    spectra_hbm,
    turning_hbm,
    currents_hbm,
    drag_hbm,
    land_hbm,
    target_hbm,
    rates_hbm,
    stokes_hbm,
    swell_hbm,
    spectra_out,
    currents_out,
    waves,
    flows,
    wave_bands,
    wave_sides,
    flow_bands,
    flow_sides,
    wave_edges,
    flow_edges,
    outgoing,
    arrived,
    half_out,
    half_in,
    unpacked,
    edge_lines,
    band_edges,
    zeros,
    no_side,
    turned,
    growths,
    spins,
    drifts,
    flow_at_waves,
    turning_ref,
    currents_ref,
    drag_ref,
    land_ref,
    target_ref,
    rates_ref,
    stokes_table,
    swell_table,
    tiny,
    turn_size,
    turn_sign,
    sea,
    load_sem,
    halo_send,
    halo_recv,
    pair_send,
    pair_recv,
):
    f32, bf16 = jnp.float32, jnp.bfloat16
    share = CELLS // sections
    sec = lax.axis_index("sec")
    lat = lax.axis_index("lat")
    has_west, has_east = sec > 0, sec < sections - 1
    has_south, has_north = lat > 0, lat < bands - 1

    lines = sections // RING
    line, spot = lax.div(sec, RING), lax.rem(sec, RING)
    hops = sorted(
        ((over, along) for over in range(lines) for along in range(RING) if over or along),
        key=lambda hop: (hop[1] == 0, -min(hop[0], lines - hop[0])),
    )

    def peer_of(hop):
        far, near = line + hop[0], spot + hop[1]
        far = jnp.where(far >= lines, far - lines, far)
        return RING * far + jnp.where(near >= RING, near - RING, near)

    peers = [peer_of(hop) for hop in hops]

    barrier = pltpu.get_barrier_semaphore()
    for peer in peers:
        pl.semaphore_signal(barrier, inc=1, device_id={"sec": peer}, device_id_type=MESH)

    for there, other in ((has_south, lat - 1), (has_north, lat + 1)):

        @pl.when(there)
        def _():
            pl.semaphore_signal(barrier, inc=1, device_id={"lat": other}, device_id_type=MESH)

    pairs = (
        (turning_hbm, turning_ref),
        (drag_hbm, drag_ref),
        (land_hbm, land_ref),
        (target_hbm, target_ref),
        (currents_hbm, currents_ref),
        (rates_hbm, rates_ref),
        (spectra_hbm, waves.at[0]),
        (stokes_hbm, stokes_table),
        (swell_hbm, swell_table),
    )
    loads = [pltpu.make_async_copy(there, here, load_sem.at[i]) for i, (there, here) in enumerate(pairs)]
    for load in loads:
        load.start()

    zeros[...] = jnp.zeros_like(zeros)
    no_side[...] = jnp.zeros_like(no_side)
    for step in range(STEPS):
        for kind, (bands_in, sides_in) in enumerate(((wave_bands, wave_sides), (flow_bands, flow_sides))):
            width = bands_in.shape[-1]
            for there, halo, k in (
                (has_west, sides_in.at[step, 0], 0),
                (has_east, sides_in.at[step, 1], 0),
                (has_south, bands_in.at[step, 0], 1),
                (has_north, bands_in.at[step, 1], 1),
            ):

                @pl.when(jnp.logical_not(there))
                def _():
                    empty = zeros.at[pl.ds(0, COLS), pl.ds(0, width)] if k else no_side.at[:, pl.ds(0, width)]
                    pltpu.make_async_copy(empty, halo, halo_recv.at[2 * step + kind, k]).start()

    tiny[...] = jnp.zeros_like(tiny)
    for load in loads[:4]:
        load.wait()
    tiny[0, 0:ROWS, 0:COLS] = turning_ref[...]
    tiny[1, 0:ROWS, 0:COLS] = land_ref[...].astype(f32)
    tiny[2, 0:ROWS, 0:COLS] = target_ref[...].astype(f32)
    tiny[3, 0:1, 0:NDEPTH] = 1.0 - drag_ref[...]

    lane_row = iota((1, 128), 1)
    target_rows = tiny[2]
    targets = jnp.full((1, 128), 99.0, f32)
    for y in range(ROWS):
        row = target_rows[y : y + 1, :]
        moved = pltpu.roll(row, COLS * y, 1) if y else row
        inside = jnp.logical_and(lane_row >= COLS * y, lane_row < COLS * (y + 1))
        targets = jnp.where(inside, moved, targets)
    matches = (iota((16, 128), 0).astype(f32) == targets).astype(f32)
    earlier = (iota((128, 128), 0) < iota((128, 128), 1)).astype(f32)
    before = jnp.dot(matches.astype(bf16), earlier.astype(bf16), preferred_element_type=f32)
    rank = jnp.sum(matches * before, axis=0, keepdims=True)
    place_of = targets * share + rank
    place = (iota((128, 128), 0).astype(f32) == place_of).astype(f32)
    place_back = jnp.transpose(place)[0:CELLS, 0:CELLS].astype(bf16)
    place = place[0:CELLS, 0:CELLS].astype(bf16)

    turn_columns = jnp.transpose(tiny[0])
    sea_columns = jnp.transpose(tiny[1])
    for y in range(ROWS):
        rows = slice(COLS * y, COLS * (y + 1))
        turn = jnp.broadcast_to(turn_columns[0:COLS, y : y + 1], (COLS, 128))
        turn_size[rows, :] = jnp.abs(turn)
        turn_sign[rows, :] = turn
        sea[rows, :] = jnp.broadcast_to(sea_columns[0:COLS, y : y + 1], (COLS, 128))

    keep = tiny[3, 0:1, :]
    keep = keep + pltpu.roll(keep, 32, 1)
    keep = keep + pltpu.roll(keep, 64, 1)

    lane = iota((COLS, 128), 1)
    column = iota((COLS, 128), 0)
    first_column = column == 0
    last_column = column == COLS - 1
    direction = lane & (NDIR - 1)
    goes_east = jnp.logical_or(direction < NDIR // 4, direction >= 3 * NDIR // 4)
    goes_north = direction < NDIR // 2
    first_direction = direction == 0
    last_direction = direction == NDIR - 1
    full_lane = iota((CELLS, 128), 1)
    low_half = full_lane < 64
    zonal = (full_lane & 63) < 32
    low_rows = iota((share // 2, 128), 1) < 64
    zonal_row = (lane & 63) < 32
    twist = jnp.where(zonal, OCEAN_DT, -OCEAN_DT)
    global_row = (lat * ROWS).astype(f32)

    def halo_copies(step, is_flow):
        bands_in, sides_in = (flow_bands, flow_sides) if is_flow else (wave_bands, wave_sides)
        edges = (flow_edges if is_flow else wave_edges).at[step]
        if is_flow:
            first = flows.at[step, pl.ds(0, COLS)]
            final = flows.at[step, pl.ds(CELLS - COLS, COLS)]
        else:
            first, final = band_edges.at[step, 0], band_edges.at[step, 1]
        index = 2 * step + is_flow
        plan = (
            (has_west, edges.at[0], sides_in.at[step, 1], 0, {"sec": sec - 1}),
            (has_east, edges.at[1], sides_in.at[step, 0], 0, {"sec": sec + 1}),
            (has_south, first, bands_in.at[step, 1], 1, {"lat": lat - 1}),
            (has_north, final, bands_in.at[step, 0], 1, {"lat": lat + 1}),
        )
        for number, (there, source, halo, k, device) in enumerate(plan):
            yield there, lambda: pltpu.make_async_remote_copy(
                src_ref=source,
                dst_ref=halo,
                send_sem=halo_send.at[index, number],
                recv_sem=halo_recv.at[index, k],
                device_id=device,
                device_id_type=MESH,
            )

    def pack(tiles, needed):
        return [
            jnp.where(needed[0 : tiles[0].shape[0]], tiles[2 * c], pltpu.roll(tiles[2 * c + 1], 16, 1))
            for c in range(SPEC // 256)
        ]

    def unpack(halo, chunk):
        return pltpu.roll(halo, 112, 1) if chunk % 2 else halo

    def half_lanes(chunk):
        return slice(128 * (chunk // 2), 128 * (chunk // 2 + 1))

    def tiles_of(values):
        return [values[:, 128 * c : 128 * (c + 1)] for c in range(SPEC // 128)]

    def ready_halos(step, is_flow):
        if is_flow:
            for y in range(ROWS):
                flow_edges[step, 0, y : y + 1, :] = flows[step, COLS * y : COLS * y + 1, :]
                flow_edges[step, 1, y : y + 1, :] = flows[step, COLS * (y + 1) - 1 : COLS * (y + 1), :]
        else:
            for y in range(ROWS):
                edge_lines[0, y : y + 1, :] = waves[step, COLS * y : COLS * y + 1, :]
                edge_lines[1, y : y + 1, :] = waves[step, COLS * (y + 1) - 1 : COLS * (y + 1), :]
            places = (
                (wave_edges, 0, edge_lines[0], jnp.logical_not(goes_east)),
                (wave_edges, 1, edge_lines[1], goes_east),
                (band_edges, 0, waves[step, 0:COLS, :], jnp.logical_not(goes_north)),
                (band_edges, 1, waves[step, CELLS - COLS : CELLS, :], goes_north),
            )
            for edges, side, values, needed in places:
                for c, tile in enumerate(pack(tiles_of(values), needed)):
                    edges[step, side, :, 128 * c : 128 * (c + 1)] = tile

    def send_halos(step, is_flow, ready=False):
        if not ready:
            ready_halos(step, is_flow)
        for there, copy in halo_copies(step, is_flow):

            @pl.when(there)
            def _():
                copy().start()

    def receive_halos(step, is_flow):
        for k, halo in enumerate((flow_sides, flow_bands) if is_flow else (wave_sides, wave_bands)):
            both = halo.at[step]
            pltpu.make_async_copy(both, both, halo_recv.at[2 * step + is_flow, k]).wait()

    def pair_copy(index, k):
        peer = peers[k]
        return pltpu.make_async_remote_copy(
            src_ref=half_out.at[index - 1, peer] if index else outgoing.at[peer],
            dst_ref=half_in.at[index - 1, sec] if index else arrived.at[sec],
            send_sem=pair_send.at[index],
            recv_sem=pair_recv.at[index],
            device_id={"sec": peer},
            device_id_type=MESH,
        )

    def start_pairs(index):
        for k in range(sections - 1):
            pair_copy(index, k).start()

    def ready_first(message):
        outgoing[...] = message.reshape(sections, share, 128)
        arrived[sec] = outgoing[sec]

    def all_pairs(index):
        others = pl.ds(0, sections - 1)
        return pltpu.make_async_remote_copy(
            src_ref=half_out.at[index - 1, others] if index else outgoing.at[others],
            dst_ref=half_in.at[index - 1, others] if index else arrived.at[others],
            send_sem=pair_send.at[index],
            recv_sem=pair_recv.at[index],
            device_id={"sec": peers[0]},
            device_id_type=MESH,
        )

    def receive(index):
        all_pairs(index).wait_recv()

    def receive_first():
        receive(0)
        return arrived[...].reshape(CELLS, 128)

    def send_pairs(index, message):
        folded = jnp.where(low_half, message, pltpu.roll(message, CELLS - share // 2, 0))
        for k in range(sections):
            half_out[index - 1, k] = folded[share * k : share * k + share // 2, :]
        start_pairs(index)
        half_in[index - 1, sec] = half_out[index - 1, sec]

    def receive_pairs(index):
        receive(index)
        for k in range(sections):
            rows = half_in[index - 1, k]
            other = pltpu.roll(rows, 64, 1)
            unpacked[index - 1, share * k : share * k + share // 2, :] = jnp.where(low_rows, rows, other)
            unpacked[index - 1, share * k + share // 2 : share * (k + 1), :] = jnp.where(low_rows, other, rows)
        return unpacked[index - 1]

    def sent_halos(step, is_flow):
        for there, copy in halo_copies(step, is_flow):

            @pl.when(there)
            def _():
                copy().wait_send()

    def sent_pairs(index):
        all_pairs(index).wait_send()

    def stokes_part(values, chunk):
        high = values.astype(bf16)
        low = (values - high.astype(f32)).astype(bf16)
        both = jnp.concatenate([high, low], axis=0)
        return jnp.dot(both, stokes_table[256 * chunk : 256 * (chunk + 1), :], preferred_element_type=f32)

    def sorted_drift(step, drift):
        drift = drift[0:CELLS] + drift[CELLS:]
        drift = drift + pltpu.roll(drift, 64, 1)
        drifts[step] = drift
        high = round_half(drift)
        pieces = jnp.where(low_half, high, drift - high).astype(bf16)
        drift = jnp.dot(place, pieces, preferred_element_type=f32)
        return drift + pltpu.roll(drift, 64, 1)

    def neighbours(own, halos, step, y, lanes, chunk=None):
        bands_in, sides_in = halos
        rows = slice(COLS * y, COLS * (y + 1))
        here = own[step, rows, lanes]
        edge = lanes if chunk is None else half_lanes(chunk)
        fit = (lambda halo: halo) if chunk is None else (lambda halo: unpack(halo, chunk))
        west = fit(sides_in[step, 0, y : y + 1, edge])
        east = fit(sides_in[step, 1, y : y + 1, edge])
        return (
            here,
            jnp.where(first_column, west, pltpu.roll(here, 1, 0)),
            jnp.where(last_column, east, pltpu.roll(here, COLS - 1, 0)),
            own[step, COLS * (y - 1) : COLS * y, lanes] if y else fit(bands_in[step, 0, :, edge]),
            own[step, COLS * (y + 1) : COLS * (y + 2), lanes]
            if y < ROWS - 1
            else fit(bands_in[step, 1, :, edge]),
        )

    def find_spin(step):
        for y in range(ROWS):
            _, west, east, south, north = neighbours(flows, (flow_bands, flow_sides), step, y, slice(0, 128))
            sheared = jnp.where(zonal_row, south - north, east - west)
            spin = 0.5 * (sheared + pltpu.roll(sheared, 32, 1))
            spins[step, COLS * y : COLS * (y + 1), :] = spin + (0.2 + 0.6 * (global_row + y) / (ROWS * bands))

    def advect(step, grown=False):
        drift = None
        for chunk in range(SPEC // 128):
            lanes = slice(128 * chunk, 128 * (chunk + 1))
            stay = rates_ref[0:1, lanes]
            rate_x = rates_ref[1:2, lanes]
            rate_y = rates_ref[2:3, lanes]
            gain = rates_ref[3:4, lanes]
            for y in range(ROWS):
                rows = slice(COLS * y, COLS * (y + 1))
                here, west, east, south, north = neighbours(
                    waves, (wave_bands, wave_sides), step, y, lanes, chunk
                )
                moved = (
                    stay * here
                    + rate_x * jnp.where(goes_east, west, east)
                    + rate_y * jnp.where(goes_north, south, north)
                )
                behind = jnp.where(first_direction, pltpu.roll(moved, 97, 1), pltpu.roll(moved, 1, 1))
                forward = jnp.where(last_direction, pltpu.roll(moved, 31, 1), pltpu.roll(moved, 127, 1))
                beside = jnp.where(turn_sign[rows, :] > 0.0, behind, forward)
                rate = turn_size[rows, :] * gain
                moved = (moved + rate * (beside - moved)) * sea[rows, :]
                if grown and step == STEPS - 1:
                    spectra_out[rows, lanes] = moved * growths[rows, lanes]
                elif grown:
                    waves[step + 1, rows, lanes] = moved * growths[rows, lanes]
                else:
                    turned[rows, lanes] = moved
            if grown and chunk % 2 and step < STEPS - 1:
                part = stokes_part(waves[step + 1, :, 128 * (chunk - 1) : 128 * (chunk + 1)], chunk // 2)
                drift = part if drift is None else drift + part
        return drift

    def push(flow, spin, drift, wet):
        return (keep * wet) * (flow + twist * spin * pltpu.roll(flow + drift, 32, 1))

    def find_growth(seen):
        seen = jnp.concatenate([seen, seen[:, 0:64]], axis=1)
        for chunk in range(SPEC // 256):
            lanes = slice(256 * chunk, 256 * (chunk + 1))
            growths[:, lanes] = 1.0 + jnp.dot(seen, swell_table[:, lanes], preferred_element_type=f32)

    def grow(seen, step):
        seen = jnp.concatenate([seen, seen[:, 0:64]], axis=1)
        for chunk in range(SPEC // 256):
            lanes = slice(256 * chunk, 256 * (chunk + 1))
            growth = jnp.dot(seen, swell_table[:, lanes], preferred_element_type=f32)
            values = turned[:, lanes] * (1.0 + growth)
            if step == STEPS:
                spectra_out[:, lanes] = values
            else:
                waves[step, :, lanes] = values
        if step == STEPS:
            return None
        send_halos(step, 0)
        return find_drift(step)

    def find_drift(step):
        drift = None
        for chunk in range(SPEC // 256):
            part = stokes_part(waves[step, :, 256 * chunk : 256 * (chunk + 1)], chunk)
            drift = part if drift is None else drift + part
        return sorted_drift(step, drift)

    def first_seen(message):
        high = round_half(message)
        pieces = jnp.where(low_half, pltpu.roll(high, 64, 1), message - high).astype(bf16)
        seen = jnp.dot(place_back, pieces, preferred_element_type=f32)
        flow_at_waves[0] = seen + pltpu.roll(seen, 64, 1)
        return seen.astype(bf16)

    def next_seen(step, message):
        high = round_half(message)
        pieces = jnp.where(low_half, high, message - high).astype(bf16)
        both = jnp.dot(place_back, pieces, preferred_element_type=f32)
        both = both + pltpu.roll(both, 64, 1)
        other = pltpu.roll(both, 32, 1)
        spin = jnp.where(zonal, both, other)
        wet = jnp.where(zonal, other, both)
        flow = push(flow_at_waves[step - 1], spin, drifts[step - 1], wet)
        flow_at_waves[step] = flow
        high = round_half(flow)
        return jnp.where(low_half, high, flow - high).astype(bf16)

    def spin_message(step):
        return jnp.where(zonal, spins[step], sea[...])

    loads[4].wait()
    start_flow = currents_ref[...].reshape(CELLS, 2 * NDEPTH)
    flows[0] = jnp.concatenate([start_flow, start_flow], axis=1)
    for load in loads[5:]:
        load.wait()
    ready_halos(0, 1)
    ready_halos(0, 0)
    ready_first(jnp.where(low_half, find_drift(0), flows[0]))

    greeted = sections - 1 + has_south.astype(jnp.int32) + has_north.astype(jnp.int32)
    pl.semaphore_wait(barrier, greeted)

    start_pairs(0)
    send_halos(0, 1, ready=True)
    send_halos(0, 0, ready=True)

    receive_halos(0, 1)
    find_spin(0)
    send_pairs(1, spin_message(0))
    receive_halos(0, 0)
    advect(0)
    message = receive_first()
    flows[1] = push(flows[0], spins[0], jnp.where(low_half, message, pltpu.roll(message, 64, 1)), sea[...])
    send_halos(1, 1)
    send_pairs(2, grow(first_seen(message), 1))

    find_growth(next_seen(1, receive_pairs(1)))
    receive_halos(1, 1)
    find_spin(1)
    send_pairs(3, spin_message(1))
    receive_halos(1, 0)
    drift = advect(1, grown=True)
    send_halos(2, 0)
    send_pairs(4, sorted_drift(2, drift))
    flows[2] = push(flows[1], spins[1], receive_pairs(2), sea[...])
    send_halos(2, 1)

    for step in range(STEPS):
        sent_halos(step, 0)
        sent_halos(step, 1)
    for index in range(2 * STEPS - 1):
        sent_pairs(index)
    find_growth(next_seen(2, receive_pairs(3)))
    receive_halos(2, 0)
    advect(2, grown=True)
    receive_halos(2, 1)
    find_spin(2)
    currents_out[...] = push(flows[2], spins[2], receive_pairs(4), sea[...])[:, 0 : 2 * NDEPTH]


def store(waves_ref, flows_ref, waves_out, flows_out, sems):
    copies = [
        pltpu.make_async_copy(waves_ref, waves_out, sems.at[0]),
        pltpu.make_async_copy(flows_ref, flows_out, sems.at[1]),
    ]
    for copy in copies:
        copy.start()
    for copy in copies:
        copy.wait()


def solution(mesh):
    sections, bands = mesh.shape["sec"], mesh.shape["lat"]
    rates, stokes_table, swell_table = build_tables()
    share = CELLS // sections

    def per_device(spectra, turning, currents, drag_rates, land_mask, ocean_target):
        f32, bf16 = jnp.float32, jnp.bfloat16
        vmem = pl.BlockSpec(memory_space=pltpu.VMEM)
        hbm = pl.BlockSpec(memory_space=pltpu.HBM)
        operands = (
            spectra.reshape(CELLS, SPEC),
            turning,
            currents,
            drag_rates.reshape(1, NDEPTH),
            land_mask,
            ocean_target,
            jnp.asarray(rates),
            jnp.asarray(stokes_table),
            jnp.asarray(swell_table),
        )
        waves, flows = pl.pallas_call(
            lambda *refs: kernel(sections, bands, *refs),
            out_shape=(
                jax.ShapeDtypeStruct((CELLS, SPEC), f32),
                jax.ShapeDtypeStruct((CELLS, 2 * NDEPTH), f32),
            ),
            in_specs=[hbm] * 9,
            out_specs=(vmem, vmem),
            scratch_shapes=[
                pltpu.VMEM((STEPS, CELLS, SPEC), f32),
                pltpu.VMEM((STEPS, CELLS, 128), f32),
                pltpu.VMEM((STEPS, 2, COLS, SPEC // 2), f32),
                pltpu.VMEM((STEPS, 2, ROWS, SPEC // 2), f32),
                pltpu.VMEM((STEPS, 2, COLS, 128), f32),
                pltpu.VMEM((STEPS, 2, ROWS, 128), f32),
                pltpu.VMEM((STEPS, 2, ROWS, SPEC // 2), f32),
                pltpu.VMEM((STEPS, 2, ROWS, 128), f32),
                pltpu.VMEM((sections, share, 128), f32),
                pltpu.VMEM((sections, share, 128), f32),
                pltpu.VMEM((2 * STEPS - 2, sections, share // 2, 128), f32),
                pltpu.VMEM((2 * STEPS - 2, sections, share // 2, 128), f32),
                pltpu.VMEM((2 * STEPS - 2, CELLS, 128), f32),
                pltpu.VMEM((2, ROWS, SPEC), f32),
                pltpu.VMEM((STEPS, 2, COLS, SPEC // 2), f32),
                pltpu.VMEM((COLS, SPEC // 2), f32),
                pltpu.VMEM((ROWS, SPEC // 2), f32),
                pltpu.VMEM((CELLS, SPEC), f32),
                pltpu.VMEM((CELLS, SPEC), f32),
                pltpu.VMEM((STEPS, CELLS, 128), f32),
                pltpu.VMEM((STEPS, CELLS, 128), f32),
                pltpu.VMEM((STEPS, CELLS, 128), f32),
                pltpu.VMEM((ROWS, COLS), f32),
                pltpu.VMEM((ROWS, COLS, 2 * NDEPTH), f32),
                pltpu.VMEM((1, NDEPTH), f32),
                pltpu.VMEM((ROWS, COLS), jnp.int32),
                pltpu.VMEM((ROWS, COLS), jnp.int32),
                pltpu.VMEM((8, SPEC), f32),
                pltpu.VMEM((SPEC, 128), bf16),
                pltpu.VMEM((6 * NDEPTH, SPEC), bf16),
                pltpu.VMEM((4, 8, 128), f32),
                pltpu.VMEM((CELLS, 128), f32),
                pltpu.VMEM((CELLS, 128), f32),
                pltpu.VMEM((CELLS, 128), f32),
                pltpu.SemaphoreType.DMA((9,)),
                pltpu.SemaphoreType.DMA((2 * STEPS, 4)),
                pltpu.SemaphoreType.DMA((2 * STEPS, 2)),
                pltpu.SemaphoreType.DMA((2 * STEPS - 1,)),
                pltpu.SemaphoreType.DMA((2 * STEPS - 1,)),
            ],
            compiler_params=pltpu.CompilerParams(
                collective_id=0, has_side_effects=True, vmem_limit_bytes=24 << 20
            ),
        )(*[pltpu.with_memory_space_constraint(x, pltpu.HBM) for x in operands])
        waves, flows = pl.pallas_call(
            store,
            out_shape=(
                jax.ShapeDtypeStruct((CELLS, SPEC), f32),
                jax.ShapeDtypeStruct((CELLS, 2 * NDEPTH), f32),
            ),
            in_specs=[vmem, vmem],
            out_specs=(hbm, hbm),
            scratch_shapes=[pltpu.SemaphoreType.DMA((2,))],
        )(*[pltpu.with_memory_space_constraint(x, pltpu.VMEM) for x in (waves, flows)])
        return waves.reshape(ROWS, COLS, SPEC), flows.reshape(ROWS, COLS, 2 * NDEPTH)

    return jax.shard_map(
        per_device,
        mesh=mesh,
        in_specs=(
            P("lat", "sec", None),
            P("lat", "sec"),
            P("lat", "sec", None),
            P(),
            P("lat", "sec"),
            P("lat", "sec"),
        ),
        out_specs=(P("lat", "sec", None), P("lat", "sec", None)),
        check_vma=False,
    )
```
